128 devices in a mesh: seq: 8 (over y, core), exp: 16 (over z, x).
Axes of the slice: x: 4, y: 4, z: 4, core: 2. Of those that a mesh axis runs over, the one named last changes fastest.
Arguments:
- queries: bfloat16 [4096, 4096], P('seq', 'exp'), may hold values from -6 to 6
- key_rows: bfloat16 [4096, 512], P('seq', 'exp'), may hold values from -6 to 6
- value_rows: bfloat16 [4096, 512], P('seq', 'exp'), may hold values from -6 to 6
- sink_logits: float32 [64], P('exp'), may hold values from 0 to 6
- out_proj: bfloat16 [4096, 2560], P('exp'), may hold values from -0.09375 to 0.09375
- residual: bfloat16 [4096, 2560], P(('seq', 'exp')), may hold values from -0.59765625 to 0.59765625
- norm_gain: float32 [2560], replicated, may hold values from 0.25 to 1.75
- expert_ids: int32 [4096, 4], P(('seq', 'exp')), may hold values from 0 to 127, all different within a row; in each aligned block of 32 rows (0 to 31, 32 to 63, ...) at most 2 rows name the same one
- gate_weights: float32 [4096, 4], P(('seq', 'exp')), may hold values from 0.2 to 1
- w_gate_up: bfloat16 [128, 2560, 2880], P(('seq', 'exp')), may hold values from -0.125 to 0.125
- w_down: bfloat16 [128, 1440, 2560], P(('seq', 'exp')), may hold values from -0.15625 to 0.15625
Outputs:
- layer_out: bfloat16 [4096, 2560], P(('seq', 'exp'))
The draws below stay inside these ranges and needn't reach their ends.
Inputs may be any that keep to these rules, and one draw needn't show every extreme that they name: `expert_ids`: each row names 4 different experts. In the rows of one device (aligned blocks of 32 rows) no expert is named more than 2 times, and in every draw some expert is named exactly 2 times in some block.
All inputs are finite; a program needn't handle non-finite values.
Results may differ from the reference program's by a relative error of at most 0.022.
Values may be sent and summed in bfloat16 or wider, within the bound.
A program may use at most 128 MiB of HBM per device.

```python
import math
import jax
import jax.numpy as jnp
import numpy as np
from jax import lax

D = 2560
FF_E = 1440
QH = 64
KVH = 8
HD = 64
WINDOW = 128
TOP = 4
TOKENS = 4096
TOK_DEV = 32
EXPERTS = 128
CAP = 2
N_EXP = 16


def draw_queries(key, part):
    drawn = jnp.clip(jax.random.normal(jax.random.fold_in(key, 1), (TOKENS, QH * HD), jnp.float32), -6.0, 6.0)
    return drawn.astype(jnp.bfloat16)


def draw_key_rows(key, part):
    drawn = jnp.clip(jax.random.normal(jax.random.fold_in(key, 2), (TOKENS, KVH * HD), jnp.float32), -6.0, 6.0)
    return drawn.astype(jnp.bfloat16)


def block_levels(stream_key, dims, pieces, low, largest):
    def one(position, parts):
        heights = jax.random.uniform(jax.random.fold_in(jax.random.fold_in(stream_key, 6), position), (parts,), jnp.float32, low / len(pieces), largest / len(pieces))
        return jnp.repeat(jnp.exp(heights), dims[position] // parts).reshape((-1,) + (1,) * (len(dims) - position - 1))

    factor_of = one(*pieces[0])
    for cut in pieces[1:]:
        factor_of = factor_of * one(*cut)
    return factor_of


def assign_block(stream_key, own, number, rows, amount, top, most, lean):
    sequence = jax.random.permutation(stream_key, amount)
    heavy_load, usual = portions_of(amount, rows * top, most, lean, True), portions_of(amount, rows * top, most, lean, False)
    places = jnp.arange(amount)

    def named(sizes, turn):
        used = int((sizes > 0).sum())
        fixed = max(1, used // 4)
        moved = fixed + (places - fixed + turn * (used - fixed)) % max(1, amount - fixed)
        return jnp.zeros((amount,), jnp.int32).at[sequence[jnp.where(places < fixed, places, moved)]].set(jnp.asarray(sizes, jnp.int32))

    sizes = jnp.where(number % 4 == 0, named(heavy_load, number // 4), named(usual, number - number // 4 - 1))
    mixed = jax.random.permutation(jax.random.fold_in(own, 3), amount)
    giver, taker = mixed[0:amount // 2 * 2:2], mixed[1:amount // 2 * 2:2]
    margin = jnp.minimum(sizes[giver] - 1, most - sizes[taker]) // 2
    margin = jnp.where((giver == sequence[0]) | (taker == sequence[0]) | (sizes[taker] == 0), 0, jnp.maximum(margin, 0))
    moved = jax.random.randint(jax.random.fold_in(own, 4), (amount // 2,), 0, 1 << 20) % (margin + 1)
    sizes = sizes.at[giver].add(-moved).at[taker].add(moved)
    labels = jnp.searchsorted(jnp.cumsum(sizes), jnp.arange(rows * top), side="right").astype(jnp.int32)
    grid = labels.reshape(top, rows).T
    grid = grid[jax.random.permutation(jax.random.fold_in(own, 1), rows)]
    turn = jax.random.randint(jax.random.fold_in(own, 2), (rows, 1), 0, top)
    return jnp.take_along_axis(grid, (jnp.arange(top)[None, :] + turn) % top, axis=1)


def portions_of(amount, total, bound, slope, full):
    weights = [(1 << 20) // math.isqrt(grade ** slope) + 1 for grade in range(1, amount + 1)]
    largest = bound if full else min(bound, max(-(-total // amount), total * weights[0] // sum(weights)))
    least = 1 if total - largest >= amount - 1 else 0
    given, spare = [largest] + [least] * (amount - 1), total - largest - least * (amount - 1)
    while spare > 0:
        candidates = [i for i in range(1, amount) if given[i] < largest] or [i for i in range(1, amount) if given[i] < bound]
        pool, budget = sum([weights[i] for i in candidates]), spare
        for i in candidates:
            addition = min(bound - given[i], max(1, budget * weights[i] // pool), spare)
            given[i] = given[i] + addition
            spare = spare - addition
    return np.array(given)


def gaussian(own_key, shape, scale, limit, pieces=(), kind=jnp.bfloat16):
    result = jax.random.normal(own_key, shape, jnp.float32) * scale
    if len(pieces) > 0:
        result = block_levels(own_key, shape, pieces, -0.22, 0.18) * result
    return jnp.clip(result, min=-limit, max=limit).astype(kind)


def setup_inputs(seed: int = 0) -> dict:
    keys = jax.random.split(jax.random.key(seed), 12)
    queries = draw_queries(jax.random.fold_in(keys[11], 71), 0)
    key_rows = draw_key_rows(jax.random.fold_in(keys[11], 71), 0)
    value_rows = gaussian(keys[2], (TOKENS, KVH * HD), 1.0, 6.0, ((0, 8), (1, 16)))
    sink_logits = jnp.clip(6.0 * jax.random.uniform(keys[3], (QH,), jnp.float32) ** block_levels(keys[3], (QH,), ((0, 16),), -0.2, 0.2), 0.0, 6.0)
    out_proj = gaussian(keys[4], (QH * HD, D), (QH * HD) ** -0.5, 0.09375, ((0, 16),))
    residual = gaussian(keys[5], (TOKENS, D), 0.1, 0.59765625, ((0, 128),))
    norm_gain = jnp.clip(1.0 + 0.15 * jax.random.normal(keys[6], (D,), jnp.float32), 0.25, 1.75)
    expert_ids_keys = jax.random.split(jax.random.fold_in(keys[7], 1), TOKENS // TOK_DEV)
    expert_ids_turns = jax.random.permutation(jax.random.fold_in(keys[7], 3), TOKENS // TOK_DEV)
    expert_ids = jax.vmap(lambda own, number: assign_block(jax.random.fold_in(keys[7], 2), own, number, TOK_DEV, EXPERTS, TOP, CAP, 2))(expert_ids_keys, expert_ids_turns).reshape((TOKENS, TOP))
    gate_weights = jnp.clip(0.2 + 0.8 * jax.random.uniform(keys[8], (TOKENS, TOP), jnp.float32) ** block_levels(keys[8], (TOKENS, TOP), ((0, 128),), -0.2, 0.2), 0.2, 1.0)
    w_gate_up = gaussian(keys[9], (EXPERTS, D, 2 * FF_E), D ** -0.5, 0.125, ((0, 128),))
    w_down = gaussian(keys[10], (EXPERTS, FF_E, D), FF_E ** -0.5, 0.15625, ((0, 128),))
    return {"queries": queries, "key_rows": key_rows, "value_rows": value_rows, "sink_logits": sink_logits, "out_proj": out_proj, "residual": residual, "norm_gain": norm_gain, "expert_ids": expert_ids, "gate_weights": gate_weights, "w_gate_up": w_gate_up, "w_down": w_down}


def window_attention(query_rows, key_block, value_block, prior_keys, prior_values, sink_row, first_index, window_size):
    row_count = query_rows.shape[0]
    head_width_dim = key_block.shape[1]
    head_count = query_rows.shape[1] // head_width_dim
    block_count = row_count // window_size
    key_ext = jnp.concatenate([prior_keys, key_block], axis=0)
    value_ext = jnp.concatenate([prior_values, value_block], axis=0)
    key_block_tiles = jnp.concatenate([key_ext[:row_count].reshape(block_count, window_size, head_width_dim), key_block.reshape(block_count, window_size, head_width_dim)], axis=1)
    value_block_tiles = jnp.concatenate([value_ext[:row_count].reshape(block_count, window_size, head_width_dim), value_block.reshape(block_count, window_size, head_width_dim)], axis=1)
    query_block_tiles = query_rows.reshape(block_count, window_size, head_count, head_width_dim)
    attention_scores = jnp.einsum('xnem,xcm->xenc', query_block_tiles.astype(jnp.float32), key_block_tiles.astype(jnp.float32)) * (1.0 / math.sqrt(head_width_dim))
    query_pos = jnp.arange(window_size, dtype=jnp.int32)[:, None]
    key_pos = jnp.arange(2 * window_size, dtype=jnp.int32)[None, :]
    inside = (key_pos > query_pos) & (key_pos <= query_pos + window_size)
    block_start = first_index + jnp.arange(block_count, dtype=jnp.int32) * window_size
    present = block_start[:, None] - window_size + key_pos >= 0
    allowed = inside[None, None, :, :] & present[:, None, None, :]
    attention_scores = jnp.where(allowed, attention_scores, -jnp.inf)
    sink_grid = sink_row.astype(jnp.float32)[None, :, None, None]
    highest = jnp.maximum(lax.optimization_barrier(jnp.max(attention_scores, axis=-1, keepdims=True)), sink_grid)
    raised = jnp.exp(attention_scores - highest)
    totals = lax.optimization_barrier(jnp.sum(raised, axis=-1, keepdims=True)) + jnp.exp(sink_grid - highest)
    attention_probabilities = (raised / totals).astype(jnp.bfloat16)
    mixed_value_rows = jnp.einsum('emjt,eta->ejma', attention_probabilities.astype(jnp.float32), value_block_tiles.astype(jnp.float32))
    return mixed_value_rows.astype(jnp.bfloat16).reshape(row_count, head_count * head_width_dim)

def expert_rows(rows_in, gate_up, down_rows):
    hidden_units = gate_up.shape[1] // 2
    both = jnp.dot(rows_in, gate_up, preferred_element_type=jnp.float32)
    gate_part = both[:, :hidden_units]
    up_part = both[:, hidden_units:]
    activated = (gate_part * jax.nn.sigmoid(1.702 * gate_part) * (up_part + 1.0)).astype(jnp.bfloat16)
    return jnp.dot(activated, down_rows, preferred_element_type=jnp.float32).astype(jnp.bfloat16)

def reference(queries, key_rows, value_rows, sink_logits, out_proj, residual, norm_gain, expert_ids, gate_weights, w_gate_up, w_down):
    total_rows = queries.shape[0]
    group_heads = QH // KVH
    query_heads = queries.reshape(total_rows, KVH, group_heads * HD).transpose(1, 0, 2)
    key_heads = key_rows.reshape(total_rows, KVH, HD).transpose(1, 0, 2)
    value_heads = value_rows.reshape(total_rows, KVH, HD).transpose(1, 0, 2)
    sink_heads = sink_logits.reshape(KVH, group_heads)
    prior_zero = jnp.zeros((WINDOW, HD), key_rows.dtype)

    def one_head(operands):
        return window_attention(operands[0], operands[1], operands[2], prior_zero, prior_zero, operands[3], 0, WINDOW)
    attended = lax.map(one_head, (query_heads, key_heads, value_heads, sink_heads))
    attended = attended.transpose(1, 0, 2).reshape(total_rows, QH * HD)
    group_width = QH * HD // N_EXP
    attn_groups = attended.reshape(total_rows, N_EXP, group_width).transpose(1, 0, 2)
    proj_groups = out_proj.reshape(N_EXP, group_width, D)

    def add_group(running, operands):
        partial_sum = jnp.dot(operands[0], operands[1], preferred_element_type=jnp.float32).astype(jnp.bfloat16)
        partial_sum = lax.optimization_barrier(partial_sum)
        return (running + partial_sum.astype(jnp.float32), None)
    projected = lax.scan(add_group, jnp.zeros((total_rows, D), jnp.float32), (attn_groups, proj_groups))[0]
    hidden = residual.astype(jnp.float32) + projected
    scale = lax.rsqrt(lax.optimization_barrier(jnp.mean(hidden * hidden, axis=-1, keepdims=True)) + 1e-05)
    normed = (hidden * scale * norm_gain.astype(jnp.float32)[None, :]).astype(jnp.bfloat16)
    flat_ids = expert_ids.reshape(-1).astype(jnp.int32)
    flat_gates = gate_weights.reshape(-1).astype(jnp.float32)
    capacity = EXPERTS * CAP
    token_of = (jnp.arange(flat_ids.shape[0], dtype=jnp.int32) // TOP).astype(jnp.int32)

    def expert_step(running, operands):
        expert_number, gate_up, down_rows = operands
        chosen = flat_ids == expert_number
        order = jnp.cumsum(chosen.astype(jnp.int32)) - 1
        slot_index = jnp.where(chosen, order, capacity).astype(jnp.int32)
        table = jnp.zeros((capacity,), jnp.int32).at[slot_index].set(token_of, mode='drop')
        slot_gates = jnp.zeros((capacity,), flat_gates.dtype).at[slot_index].set(flat_gates, mode='drop')
        outputs = expert_rows(normed[table], gate_up, down_rows)
        running = running.at[table].add(slot_gates[:, None] * outputs.astype(jnp.float32))
        return (running, None)
    combined = lax.scan(expert_step, hidden, (jnp.arange(EXPERTS, dtype=jnp.int32), w_gate_up, w_down))[0]
    return combined.astype(jnp.bfloat16)
```

```python
import math

import jax
import jax.numpy as jnp
from jax import lax
from jax.experimental import pallas as pl
from jax.experimental.pallas import tpu as pltpu
from jax.sharding import PartitionSpec as P

MESH = pl.DeviceIdType.MESH
BF = jnp.bfloat16
F32 = jnp.float32
D = 2560
H = 1280
FF = 1440
COL = 256


def mm(a, b):
    return jnp.dot(a, b, preferred_element_type=F32)


def mm_nt(a, b):
    return lax.dot_general(a, b, (((1,), (1,)), ((), ())), preferred_element_type=F32)


def mm_tn(a, b):
    return lax.dot_general(a, b, (((0,), (0,)), ((), ())), preferred_element_type=F32)


def remote(src, dst, send_sem, recv_sem, device):
    return pltpu.make_async_remote_copy(
        src, dst, send_sem, recv_sem, device_id=device, device_id_type=MESH
    )


def aligned(value, multiple):
    return pl.multiple_of(value, multiple)


def loop(low, high, body):
    def step(i, carry):
        body(i)
        return carry

    lax.fori_loop(low, high, step, 0)


def layer_kernel(
    q_hbm, k_hbm, v_hbm, sink_ref, wo_hbm, res_hbm, gain_ref, ids_ref, gates_ref, wgu_hbm, wd_hbm,
    out_ref,
    q, kraw, vraw, wo, res, wgu, wd,
    kext, bdk, bdv, att,
    part_a, part_b, recv_z, recv_x, sum_a, sum_b, recv_a2, recv_b2,
    hidden, normed, dsel, wsel, perm,
    da1, db1, ra1, rb1, da2, db2, ra2, rb2, xb,
    both, act,
    ta1, yb, tb1, ua1, ub1, ta2, tb2, ua2, ub2,
    load_sem, kv_send, kv_recv, z_send, z_recv, x_send, x_recv, a2_send, a2_recv, b2_send, b2_recv,
    ex_send, ex_recv, sq_send, sq_recv,
):
    s = lax.axis_index("seq")
    e = lax.axis_index("exp")
    z = e // 4
    x = lax.rem(e, 4)
    parity = lax.rem(e, 2)
    mate = e + 1 - 2 * parity
    s_next = lax.rem(s + 1, 8)
    s_last = lax.rem(s + 7, 8)

    loads = [
        pltpu.make_async_copy(a, b, load_sem.at[i])
        for i, (a, b) in enumerate(
            [(k_hbm, kraw), (v_hbm, vraw), (q_hbm, q), (wo_hbm, wo), (res_hbm, res), (wgu_hbm, wgu), (wd_hbm, wd)]
        )
    ]
    for c in loads:
        c.start()

    barrier = pltpu.get_barrier_semaphore()

    def greet(device):
        pl.semaphore_signal(barrier, inc=1, device_id=device, device_id_type=MESH)

    loop(1, 16, lambda d: greet((s, lax.rem(e + d, 16))))
    loop(1, 8, lambda d: greet((lax.rem(s + d, 8), e)))
    greet((s_next, mate))
    greet((s_last, mate))

    eye = (
        lax.broadcasted_iota(jnp.int32, (32, 32), 0) == lax.broadcasted_iota(jnp.int32, (32, 32), 1)
    ).astype(F32).astype(BF)
    loads[0].wait()
    kext[parity, 0:32, 128:640] = mm_nt(eye, kraw[...]).astype(BF)
    loads[1].wait()
    kext[parity, 32:64, 128:640] = mm_nt(eye, vraw[...]).astype(BF)
    pl.semaphore_wait(barrier, 24)
    own_rows = kext.at[parity, :, pl.ds(128, 512)]
    own_tail = kext.at[parity, :, pl.ds(512, 128)]
    prior = kext.at[parity, :, pl.ds(0, 128)]
    kv_copies = [
        remote(own_rows, own_rows, kv_send.at[0], kv_recv.at[0], (s, mate)),
        remote(own_tail, prior, kv_send.at[1], kv_recv.at[1], (s_next, e)),
        remote(own_tail, prior, kv_send.at[2], kv_recv.at[2], (s_next, mate)),
    ]
    for c in kv_copies:
        c.start()

    ids = ids_ref[...]
    gates = gates_ref[...]
    before = (
        lax.broadcasted_iota(jnp.int32, (32, 32), 1) < lax.broadcasted_iota(jnp.int32, (32, 32), 0)
    ).astype(F32).astype(BF)
    lane = lax.broadcasted_iota(jnp.int32, (32, 256), 1)
    slot = (lane & 1).astype(F32)
    for order in range(2):
        expert = ((lane & 15) >> 1) * 16 + (lane >> 4) if order == 0 else lane >> 1
        named = jnp.zeros((32, 256), F32)
        weight = jnp.zeros((32, 256), F32)
        for k in range(4):
            same = ids[:, k : k + 1] == expert
            named = named + jnp.where(same, 1.0, 0.0)
            weight = weight + jnp.where(same, gates[:, k : k + 1], 0.0)
        rank = mm(before, named.astype(BF))
        chosen = jnp.where(rank == slot, named, 0.0)
        dsel[order] = chosen.astype(BF)
        weight = weight * chosen
        high = weight.astype(BF)
        wsel[order, 0:32, :] = high
        wsel[order, 32:64, :] = (weight - high.astype(F32)).astype(BF)
    row = lax.broadcasted_iota(jnp.int32, (256, 256), 0)
    col = lax.broadcasted_iota(jnp.int32, (256, 256), 1)
    to = ((row & 31) >> 1) * 16 + (row >> 5) * 2 + (row & 1)
    back = ((row & 15) >> 1) * 32 + (row >> 4) * 2 + (row & 1)
    perm[0] = jnp.where(col == to, 1.0, 0.0).astype(BF)
    perm[1] = jnp.where(col == back, 1.0, 0.0).astype(BF)

    bdk[...] = jnp.zeros((128, 512), BF)
    bdv[...] = jnp.zeros((128, 512), BF)
    loads[2].wait()
    loads[3].wait()
    for c in kv_copies:
        c.wait_recv()

    def z_copy(i):
        b = lax.rem(z + 1 + i, 4)
        return remote(part_a.at[b], recv_z.at[z], z_send.at[i], z_recv.at[i], (s, b * 4 + x))

    def x_copy(d, i):
        b = lax.rem(z + 1 + i, 4)
        other = lax.rem(x + 1 + d, 4)
        return remote(
            part_b.at[b, pl.ds(aligned(other * 32, 32), 32)],
            recv_x.at[x, b],
            x_send.at[d, i],
            x_recv.at[d, i],
            (s, z * 4 + other),
        )

    query_pos = lax.broadcasted_iota(jnp.int32, (128, 256), 0)
    key_pos = lax.broadcasted_iota(jnp.int32, (128, 256), 1)
    inside = (key_pos > query_pos) & (key_pos <= query_pos + 128)

    def attend(i):
        b = lax.rem(z + 1 + i, 4)
        window = pl.ds(aligned(b * 128, 128), 256)
        for half in range(2):
            for p in range(2):
                rows = slice(half * 64 + p * 32, half * 64 + p * 32 + 32)
                bdk[rows, half * 256 : half * 256 + 256] = kext[p, 0:32, window]
                bdv[rows, half * 256 : half * 256 + 256] = kext[p, 32:64, window]
        allowed = inside & (key_pos + (s * 512 + b * 128) >= 128)
        for pair in range(2):
            queries = q[pl.ds(aligned(b * 128, 128), 128), pair * 128 : pair * 128 + 128]
            scores = mm(queries, bdk[...]) * (1.0 / math.sqrt(64))
            probs = []
            for half in range(2):
                sink = sink_ref[pair * 2 + half]
                part = jnp.where(allowed, scores[:, half * 256 : half * 256 + 256], -1e30)
                highest = jnp.maximum(jnp.max(part, axis=1, keepdims=True), sink)
                raised = jnp.exp(part - highest)
                total = jnp.sum(raised, axis=1, keepdims=True) + jnp.exp(sink - highest)
                probs.append((raised * (1.0 / total)).astype(BF))
            mixed = mm_nt(jnp.concatenate(probs, axis=1), bdv[...])
            att[:, pair * 128 : pair * 128 + 128] = mixed.astype(BF)
        attended = att[...]
        for n in range(5):
            part_a[b, :, n * COL : n * COL + COL] = mm(attended, wo[:, n * COL : n * COL + COL]).astype(BF)

        @pl.when(i < 3)
        def _():
            z_copy(i).start()

        for n in range(5):
            part_b[b, :, n * COL : n * COL + COL] = mm(
                attended, wo[:, H + n * COL : H + n * COL + COL]
            ).astype(BF)
        for d in range(3):
            x_copy(d, i).start()

    loop(0, 4, attend)

    def a2_copy(i):
        other = lax.rem(x + 1 + i, 4)
        return remote(
            sum_a.at[pl.ds(aligned(other * 32, 32), 32)],
            recv_a2.at[x],
            a2_send.at[i],
            a2_recv.at[i],
            (s, z * 4 + other),
        )

    def b2_copy(i):
        b = lax.rem(z + 1 + i, 4)
        return remote(sum_b.at[b], recv_b2.at[z], b2_send.at[i], b2_recv.at[i], (s, b * 4 + x))

    for i in range(3):
        z_copy(i).wait_recv()

    def sum_over_z(i):
        other = lax.rem(x + 1 + i, 4)
        rows = pl.ds(aligned(other * 32, 32), 32)
        total = part_a[z, rows, :].astype(F32)
        for d in range(1, 4):
            total = total + recv_z[lax.rem(z + d, 4), rows, :].astype(F32)
        sum_a[rows, :] = total.astype(BF)

        @pl.when(i < 3)
        def _():
            a2_copy(i).start()

    loop(0, 4, sum_over_z)

    def sum_over_x(i):
        b = lax.rem(z + 1 + i, 4)
        for d in range(3):
            x_copy(d, i).wait_recv()
        total = part_b[b, pl.ds(aligned(x * 32, 32), 32), :].astype(F32)
        for d in range(1, 4):
            total = total + recv_x[lax.rem(x + d, 4), b].astype(F32)
        sum_b[b] = total.astype(BF)

        @pl.when(i < 3)
        def _():
            b2_copy(i).start()

    loop(0, 4, sum_over_x)

    loads[4].wait()
    for i in range(3):
        a2_copy(i).wait_recv()
    total = sum_a[pl.ds(aligned(x * 32, 32), 32), :].astype(F32)
    for d in range(1, 4):
        total = total + recv_a2[lax.rem(x + d, 4)].astype(F32)
    hidden_a = res[:, 0:H].astype(F32) + total
    hidden[:, 0:H] = hidden_a
    for i in range(3):
        b2_copy(i).wait_recv()
    total = sum_b[z].astype(F32)
    for d in range(1, 4):
        total = total + recv_b2[lax.rem(z + d, 4)].astype(F32)
    hidden_b = res[:, H:D].astype(F32) + total
    hidden[:, H:D] = hidden_b
    squares = jnp.sum(hidden_a * hidden_a, axis=1, keepdims=True) + jnp.sum(
        hidden_b * hidden_b, axis=1, keepdims=True
    )
    scale = lax.rsqrt(squares * (1.0 / D) + 1e-05)
    normed[:, 0:H] = (hidden[:, 0:H] * scale * gain_ref[:, 0:H]).astype(BF)
    normed[:, H:D] = (hidden[:, H:D] * scale * gain_ref[:, H:D]).astype(BF)

    def ex_copy(use, src, dst, d):
        g = lax.rem(e + d, 16)
        return remote(
            src.at[pl.ds(aligned(g * 16, 16), 16)],
            dst.at[pl.ds(aligned(e * 16, 16), 16)],
            ex_send.at[use, d - 1],
            ex_recv.at[use, d - 1],
            (s, g),
        )

    def sq_copy(use, src, dst, d):
        g = lax.rem(s + d, 8)
        return remote(
            src.at[pl.ds(aligned(g * 32, 32), 32)],
            dst.at[pl.ds(aligned(s * 32, 32), 32)],
            sq_send.at[use, d - 1],
            sq_recv.at[use, d - 1],
            (g, e),
        )

    def ex_start(use, src, dst):
        loop(1, 16, lambda d: ex_copy(use, src, dst, d).start())
        own = pl.ds(aligned(e * 16, 16), 16)
        dst[own, :] = src[own, :]

    def ex_wait(use, src, dst):
        loop(1, 16, lambda d: ex_copy(use, src, dst, d).wait_recv())

    def sq_start(use, src, dst):
        loop(1, 8, lambda d: sq_copy(use, src, dst, d).start())
        own = pl.ds(aligned(s * 32, 32), 32)
        dst[own, :] = src[own, :]

    def sq_wait(use, src, dst):
        loop(1, 8, lambda d: sq_copy(use, src, dst, d).wait_recv())

    def chunk(n, base=0):
        return pl.ds(aligned(base + n * COL, COL), COL)

    def permute(which, src, dst):
        def step(n):
            dst[:, chunk(n)] = mm(perm[which], src[:, chunk(n)]).astype(BF)

        loop(0, 5, step)

    def place_a(n):
        da1[:, chunk(n)] = mm_tn(dsel[0], normed[:, chunk(n)]).astype(BF)

    def place_b(n):
        db1[:, chunk(n)] = mm_tn(dsel[1], normed[:, chunk(n, H)]).astype(BF)

    loop(0, 5, place_a)
    ex_start(0, da1, ra1)
    loop(0, 5, place_b)
    sq_start(0, db1, rb1)
    ex_wait(0, da1, ra1)
    permute(0, ra1, da2)
    sq_start(1, da2, ra2)
    sq_wait(0, db1, rb1)
    permute(1, rb1, db2)
    ex_start(1, db2, rb2)
    sq_wait(1, da2, ra2)
    ex_wait(1, db2, rb2)
    permute(0, rb2, xb)

    loads[5].wait()

    def up(n):
        both[:, chunk(n)] = mm(ra2[...], wgu[0, 0:H, chunk(n)]) + mm(xb[...], wgu[0, H:D, chunk(n)])

    loop(0, 11, up)
    both[:, 2816:2880] = mm(ra2[...], wgu[0, 0:H, 2816:2880]) + mm(xb[...], wgu[0, H:D, 2816:2880])

    def activate(r):
        rows = pl.ds(aligned(r * 32, 32), 32)
        gate = both[rows, 0:FF]
        lift = both[rows, FF : 2 * FF]
        act[rows, :] = (gate * (1.0 / (1.0 + jnp.exp(-1.702 * gate))) * (lift + 1.0)).astype(BF)

    loop(0, 8, activate)
    loads[6].wait()

    def down_a(n):
        ta1[:, chunk(n)] = mm(act[...], wd[0, :, chunk(n)]).astype(BF)

    def down_b(n):
        yb[:, chunk(n)] = mm(act[...], wd[0, :, chunk(n, H)]).astype(BF)

    loop(0, 5, down_a)
    sq_start(2, ta1, ua1)
    loop(0, 5, down_b)
    permute(1, yb, tb1)
    ex_start(2, tb1, ub1)
    sq_wait(2, ta1, ua1)
    permute(1, ua1, ta2)
    ex_start(3, ta2, ua2)
    ex_wait(2, tb1, ub1)
    permute(0, ub1, tb2)
    sq_start(3, tb2, ub2)

    def combine(order, src, base, n):
        weighted = mm(wsel[order], src[:, chunk(n)])
        out_ref[:, chunk(n, base)] = (hidden[:, chunk(n, base)] + weighted[0:32] + weighted[32:64]).astype(BF)

    ex_wait(3, ta2, ua2)
    loop(0, 5, lambda n: combine(0, ua2, 0, n))
    sq_wait(3, tb2, ub2)
    loop(0, 5, lambda n: combine(1, ub2, H, n))

    for c in kv_copies:
        c.wait_send()
    for i in range(3):
        z_copy(i).wait_send()
        a2_copy(i).wait_send()
        b2_copy(i).wait_send()
        loop(0, 4, lambda j: x_copy(i, j).wait_send())
    for use, src, dst in ((0, da1, ra1), (1, db2, rb2), (2, tb1, ub1), (3, ta2, ua2)):
        loop(1, 16, lambda d: ex_copy(use, src, dst, d).wait_send())
    for use, src, dst in ((0, db1, rb1), (1, da2, ra2), (2, ta1, ua1), (3, tb2, ub2)):
        loop(1, 8, lambda d: sq_copy(use, src, dst, d).wait_send())


def per_device(
    queries, key_rows, value_rows, sink_logits, out_proj, residual, norm_gain, expert_ids, gate_weights,
    w_gate_up, w_down,
):
    hbm = pl.BlockSpec(memory_space=pl.ANY)
    vmem = pl.BlockSpec(memory_space=pltpu.VMEM)
    smem = pl.BlockSpec(memory_space=pltpu.SMEM)
    dma = pltpu.SemaphoreType.DMA
    wide = pltpu.VMEM((256, H), BF)
    scratch = [
        pltpu.VMEM((512, 256), BF),
        pltpu.VMEM((512, 32), BF),
        pltpu.VMEM((512, 32), BF),
        pltpu.VMEM((256, D), BF),
        pltpu.VMEM((32, D), BF),
        pltpu.VMEM((1, D, 2 * FF), BF),
        pltpu.VMEM((1, FF, D), BF),
        pltpu.VMEM((2, 64, 640), BF),
        pltpu.VMEM((128, 512), BF),
        pltpu.VMEM((128, 512), BF),
        pltpu.VMEM((128, 256), BF),
        pltpu.VMEM((4, 128, H), BF),
        pltpu.VMEM((4, 128, H), BF),
        pltpu.VMEM((4, 128, H), BF),
        pltpu.VMEM((4, 4, 32, H), BF),
        pltpu.VMEM((128, H), BF),
        pltpu.VMEM((4, 32, H), BF),
        pltpu.VMEM((4, 32, H), BF),
        pltpu.VMEM((4, 32, H), BF),
        pltpu.VMEM((32, D), F32),
        pltpu.VMEM((32, D), BF),
        pltpu.VMEM((2, 32, 256), BF),
        pltpu.VMEM((2, 64, 256), BF),
        pltpu.VMEM((2, 256, 256), BF),
        *[wide] * 9,
        pltpu.VMEM((256, 2 * FF), F32),
        pltpu.VMEM((256, FF), BF),
        *[wide] * 9,
        dma((7,)),
        dma((3,)),
        dma((3,)),
        dma((3,)),
        dma((3,)),
        dma((3, 4)),
        dma((3, 4)),
        dma((3,)),
        dma((3,)),
        dma((3,)),
        dma((3,)),
        dma((4, 15)),
        dma((4, 15)),
        dma((4, 7)),
        dma((4, 7)),
    ]
    return pl.pallas_call(
        layer_kernel,
        out_shape=jax.ShapeDtypeStruct((32, D), BF),
        in_specs=[hbm, hbm, hbm, smem, hbm, hbm, vmem, vmem, vmem, hbm, hbm],
        out_specs=vmem,
        scratch_shapes=scratch,
        compiler_params=pltpu.CompilerParams(
            collective_id=1, has_side_effects=True, vmem_limit_bytes=60 * 1024 * 1024
        ),
        name="layer",
    )(
        queries, key_rows, value_rows, sink_logits, out_proj, residual, norm_gain.reshape(1, D),
        expert_ids, gate_weights, w_gate_up, w_down,
    )


def solution(mesh):
    return jax.shard_map(
        per_device,
        mesh=mesh,
        in_specs=(
            P("seq", "exp"),
            P("seq", "exp"),
            P("seq", "exp"),
            P("exp"),
            P("exp", None),
            P(("seq", "exp"), None),
            P(),
            P(("seq", "exp"), None),
            P(("seq", "exp"), None),
            P(("seq", "exp"), None, None),
            P(("seq", "exp"), None, None),
        ),
        out_specs=P(("seq", "exp"), None),
        check_vma=False,
    )
```

```python
import math

import jax
import jax.numpy as jnp
from jax import lax
from jax.experimental import pallas as pl
from jax.experimental.pallas import tpu as pltpu
from jax.sharding import PartitionSpec as P

MESH = pl.DeviceIdType.MESH
BF = jnp.bfloat16
F32 = jnp.float32
D = 2560
H = 1280
FF = 1440
COL = 256


def mm(a, b):
    return jnp.dot(a, b, preferred_element_type=F32)


def mm_nt(a, b):
    return lax.dot_general(a, b, (((1,), (1,)), ((), ())), preferred_element_type=F32)


def remote(src, dst, send_sem, recv_sem, device):
    return pltpu.make_async_remote_copy(
        src, dst, send_sem, recv_sem, device_id=device, device_id_type=MESH
    )


def aligned(value, multiple):
    return pl.multiple_of(value, multiple)


def loop(low, high, body):
    def step(i, carry):
        body(i)
        return carry

    lax.fori_loop(low, high, step, 0)


def layer_kernel(
    q_hbm, k_hbm, v_hbm, sink_ref, wo_hbm, res_hbm, gain_ref, ids_ref, gates_ref, wgu_hbm, wd_hbm,
    out_ref,
    q, kraw, vraw, wo, res, wgu, wd,
    kext, bdk, bdv, att,
    part_a, part_b, recv_z, recv_x, sum_a, sum_b, recv_a2, recv_b2,
    hidden, normed, dsel, wsel, perm,
    da1, db1, ra1, rb1, da2, db2, ra2, rb2, xb,
    act,
    ta1, yb, tb1, ua1, ub1, ta2, tb2, ua2, ub2,
    load_sem, kv_send, kv_recv, z_send, z_recv, x_send, x_recv, a2_send, a2_recv, b2_send, b2_recv,
    ex_send, ex_recv, sq_send, sq_recv,
):
    s = lax.axis_index("seq")
    e = lax.axis_index("exp")
    z = e // 4
    x = lax.rem(e, 4)
    parity = lax.rem(e, 2)
    mate = e + 1 - 2 * parity
    s_next = lax.rem(s + 1, 8)
    s_last = lax.rem(s + 7, 8)

    loads = [
        pltpu.make_async_copy(a, b, load_sem.at[i])
        for i, (a, b) in enumerate(
            [(k_hbm, kraw), (v_hbm, vraw), (q_hbm, q), (wo_hbm, wo), (res_hbm, res), (wgu_hbm, wgu), (wd_hbm, wd)]
        )
    ]
    for c in loads:
        c.start()

    barrier = pltpu.get_barrier_semaphore()

    def greet(device):
        pl.semaphore_signal(barrier, inc=1, device_id=device, device_id_type=MESH)

    loop(1, 16, lambda d: greet((s, lax.rem(e + d, 16))))
    loop(1, 8, lambda d: greet((lax.rem(s + d, 8), e)))
    greet((s_next, mate))
    greet((s_last, mate))

    loads[0].wait()
    kext[parity, 0:32, 128:640] = kraw[...]
    loads[1].wait()
    kext[parity, 32:64, 128:640] = vraw[...]
    pl.semaphore_wait(barrier, 24)
    own_rows = kext.at[parity, :, pl.ds(128, 512)]
    own_tail = kext.at[parity, :, pl.ds(512, 128)]
    prior = kext.at[parity, :, pl.ds(0, 128)]
    kv_copies = [
        remote(own_rows, own_rows, kv_send.at[0], kv_recv.at[0], (s, mate)),
        remote(own_tail, prior, kv_send.at[1], kv_recv.at[1], (s_next, e)),
        remote(own_tail, prior, kv_send.at[2], kv_recv.at[2], (s_next, mate)),
    ]
    for c in kv_copies:
        c.start()

    ids = ids_ref[...]
    gates = gates_ref[...]
    before = (
        lax.broadcasted_iota(jnp.int32, (32, 32), 0) < lax.broadcasted_iota(jnp.int32, (32, 32), 1)
    ).astype(F32).astype(BF)
    place = lax.broadcasted_iota(jnp.int32, (256, 32), 0)
    slot = (place & 1).astype(F32)
    for order in range(2):
        expert = ((place & 15) >> 1) * 16 + (place >> 4) if order == 0 else place >> 1
        named = jnp.zeros((256, 32), F32)
        weight = jnp.zeros((256, 32), F32)
        for k in range(4):
            same = ids[k : k + 1, :] == expert
            named = named + jnp.where(same, 1.0, 0.0)
            weight = weight + jnp.where(same, gates[k : k + 1, :], 0.0)
        rank = mm(named.astype(BF), before)
        chosen = jnp.where(rank == slot, named, 0.0)
        dsel[order] = chosen.astype(BF)
        weight = jnp.transpose(weight * chosen)
        high = weight.astype(BF)
        wsel[order, 0:32, :] = high
        wsel[order, 32:64, :] = (weight - high.astype(F32)).astype(BF)
    row = lax.broadcasted_iota(jnp.int32, (256, 256), 0)
    col = lax.broadcasted_iota(jnp.int32, (256, 256), 1)
    to = ((row & 31) >> 1) * 16 + (row >> 5) * 2 + (row & 1)
    back = ((row & 15) >> 1) * 32 + (row >> 4) * 2 + (row & 1)
    perm[0] = jnp.where(col == to, 1.0, 0.0).astype(BF)
    perm[1] = jnp.where(col == back, 1.0, 0.0).astype(BF)

    bdk[...] = jnp.zeros((128, 512), BF)
    bdv[...] = jnp.zeros((128, 512), BF)
    loads[2].wait()
    loads[3].wait()
    for c in kv_copies:
        c.wait_recv()

    def z_copy(i):
        b = lax.rem(z + 1 + i, 4)
        return remote(part_a.at[b], recv_z.at[z], z_send.at[i], z_recv.at[i], (s, b * 4 + x))

    def x_copy(d, i):
        b = lax.rem(z + 1 + i, 4)
        other = lax.rem(x + 1 + d, 4)
        return remote(
            part_b.at[b, pl.ds(aligned(other * 32, 32), 32)],
            recv_x.at[x, b],
            x_send.at[d, i],
            x_recv.at[d, i],
            (s, z * 4 + other),
        )

    query_pos = lax.broadcasted_iota(jnp.int32, (128, 256), 0)
    key_pos = lax.broadcasted_iota(jnp.int32, (128, 256), 1)
    inside = (key_pos > query_pos) & (key_pos <= query_pos + 128)

    def attend(i):
        b = lax.rem(z + 1 + i, 4)
        window = pl.ds(aligned(b * 128, 128), 256)
        for half in range(2):
            for p in range(2):
                rows = slice(half * 64 + p * 32, half * 64 + p * 32 + 32)
                bdk[rows, half * 256 : half * 256 + 256] = kext[p, 0:32, window]
                bdv[rows, half * 256 : half * 256 + 256] = kext[p, 32:64, window]
        allowed = inside & (key_pos + (s * 512 + b * 128) >= 128)
        for pair in range(2):
            queries = q[pl.ds(aligned(b * 128, 128), 128), pair * 128 : pair * 128 + 128]
            scores = mm(queries, bdk[...]) * (1.0 / math.sqrt(64))
            probs = []
            for half in range(2):
                sink = sink_ref[pair * 2 + half]
                part = jnp.where(allowed, scores[:, half * 256 : half * 256 + 256], -1e30)
                highest = jnp.maximum(jnp.max(part, axis=1, keepdims=True), sink)
                raised = jnp.exp(part - highest)
                total = jnp.sum(raised, axis=1, keepdims=True) + jnp.exp(sink - highest)
                probs.append((raised * (1.0 / total)).astype(BF))
            mixed = mm_nt(jnp.concatenate(probs, axis=1), bdv[...])
            att[:, pair * 128 : pair * 128 + 128] = mixed.astype(BF)
        attended = att[...]
        for n in range(5):
            part_a[b, :, n * COL : n * COL + COL] = mm(attended, wo[:, n * COL : n * COL + COL]).astype(BF)

        @pl.when(i < 3)
        def _():
            z_copy(i).start()

        for n in range(5):
            part_b[b, :, n * COL : n * COL + COL] = mm(
                attended, wo[:, H + n * COL : H + n * COL + COL]
            ).astype(BF)
        for d in range(3):
            x_copy(d, i).start()

    loop(0, 4, attend)

    def a2_copy(i):
        other = lax.rem(x + 1 + i, 4)
        return remote(
            sum_a.at[pl.ds(aligned(other * 32, 32), 32)],
            recv_a2.at[x],
            a2_send.at[i],
            a2_recv.at[i],
            (s, z * 4 + other),
        )

    def b2_copy(i):
        b = lax.rem(z + 1 + i, 4)
        return remote(sum_b.at[b], recv_b2.at[z], b2_send.at[i], b2_recv.at[i], (s, b * 4 + x))

    for i in range(3):
        z_copy(i).wait_recv()

    def sum_over_z(i):
        other = lax.rem(x + 1 + i, 4)
        rows = pl.ds(aligned(other * 32, 32), 32)
        total = part_a[z, rows, :].astype(F32)
        for d in range(1, 4):
            total = total + recv_z[lax.rem(z + d, 4), rows, :].astype(F32)
        sum_a[rows, :] = total.astype(BF)

        @pl.when(i < 3)
        def _():
            a2_copy(i).start()

    loop(0, 4, sum_over_z)

    def sum_over_x(i):
        b = lax.rem(z + 1 + i, 4)
        for d in range(3):
            x_copy(d, i).wait_recv()
        total = part_b[b, pl.ds(aligned(x * 32, 32), 32), :].astype(F32)
        for d in range(1, 4):
            total = total + recv_x[lax.rem(x + d, 4), b].astype(F32)
        sum_b[b] = total.astype(BF)

        @pl.when(i < 3)
        def _():
            b2_copy(i).start()

    loop(0, 4, sum_over_x)

    loads[4].wait()
    for i in range(3):
        a2_copy(i).wait_recv()
    total = sum_a[pl.ds(aligned(x * 32, 32), 32), :].astype(F32)
    for d in range(1, 4):
        total = total + recv_a2[lax.rem(x + d, 4)].astype(F32)
    hidden_a = res[:, 0:H].astype(F32) + total
    hidden[:, 0:H] = hidden_a
    for i in range(3):
        b2_copy(i).wait_recv()
    total = sum_b[z].astype(F32)
    for d in range(1, 4):
        total = total + recv_b2[lax.rem(z + d, 4)].astype(F32)
    hidden_b = res[:, H:D].astype(F32) + total
    hidden[:, H:D] = hidden_b
    squares = jnp.sum(hidden_a * hidden_a, axis=1, keepdims=True) + jnp.sum(
        hidden_b * hidden_b, axis=1, keepdims=True
    )
    scale = lax.rsqrt(squares * (1.0 / D) + 1e-05)
    normed[...] = (hidden[...] * scale * gain_ref[...].reshape(1, D)).astype(BF)

    def ex_copy(use, src, dst, d):
        g = lax.rem(e + d, 16)
        return remote(
            src.at[pl.ds(aligned(g * 16, 16), 16)],
            dst.at[pl.ds(aligned(e * 16, 16), 16)],
            ex_send.at[use, d - 1],
            ex_recv.at[use, d - 1],
            (s, g),
        )

    def sq_copy(use, src, dst, d):
        g = lax.rem(s + d, 8)
        return remote(
            src.at[pl.ds(aligned(g * 32, 32), 32)],
            dst.at[pl.ds(aligned(s * 32, 32), 32)],
            sq_send.at[use, d - 1],
            sq_recv.at[use, d - 1],
            (g, e),
        )

    def ex_start(use, src, dst):
        loop(1, 16, lambda d: ex_copy(use, src, dst, d).start())
        own = pl.ds(aligned(e * 16, 16), 16)
        dst[own, :] = src[own, :]

    def ex_wait(use, src, dst):
        loop(1, 16, lambda d: ex_copy(use, src, dst, d).wait_recv())

    def sq_start(use, src, dst):
        loop(1, 8, lambda d: sq_copy(use, src, dst, d).start())
        own = pl.ds(aligned(s * 32, 32), 32)
        dst[own, :] = src[own, :]

    def sq_wait(use, src, dst):
        loop(1, 8, lambda d: sq_copy(use, src, dst, d).wait_recv())

    def chunk(n, base=0):
        return pl.ds(aligned(base + n * COL, COL), COL)

    def permute(which, src, dst):
        def step(n):
            dst[:, chunk(n)] = mm(perm[which], src[:, chunk(n)]).astype(BF)

        loop(0, 5, step)

    def place_a(n):
        da1[:, chunk(n)] = mm(dsel[0], normed[:, chunk(n)]).astype(BF)

    def place_b(n):
        db1[:, chunk(n)] = mm(dsel[1], normed[:, chunk(n, H)]).astype(BF)

    loop(0, 5, place_a)
    ex_start(0, da1, ra1)
    loop(0, 5, place_b)
    sq_start(0, db1, rb1)
    ex_wait(0, da1, ra1)
    permute(0, ra1, da2)
    sq_start(1, da2, ra2)
    sq_wait(0, db1, rb1)
    permute(1, rb1, db2)
    ex_start(1, db2, rb2)
    sq_wait(1, da2, ra2)
    ex_wait(1, db2, rb2)
    permute(0, rb2, xb)

    loads[5].wait()

    def up(n, width):
        rows = pl.ds(aligned(n * width, 16), width)
        lift_rows = pl.ds(aligned(FF + n * width, 16), width)
        pieces = []
        for r in (rows, lift_rows):
            pieces.append(mm_nt(ra2[...], wgu[0, r, 0:H]) + mm_nt(xb[...], wgu[0, r, H:D]))
        gate, lift = pieces
        act[:, n * width : n * width + width] = (
            gate * (1.0 / (1.0 + jnp.exp(-1.702 * gate))) * (lift + 1.0)
        ).astype(BF)

    for n in range(5):
        up(n, 256)
    up(8, 160)
    loads[6].wait()

    def down_a(n):
        ta1[:, chunk(n)] = mm(act[...], wd[0, :, chunk(n)]).astype(BF)

    def down_b(n):
        yb[:, chunk(n)] = mm(act[...], wd[0, :, chunk(n, H)]).astype(BF)

    loop(0, 5, down_a)
    sq_start(2, ta1, ua1)
    loop(0, 5, down_b)
    permute(1, yb, tb1)
    ex_start(2, tb1, ub1)
    sq_wait(2, ta1, ua1)
    permute(1, ua1, ta2)
    ex_start(3, ta2, ua2)
    ex_wait(2, tb1, ub1)
    permute(0, ub1, tb2)
    sq_start(3, tb2, ub2)

    def combine(order, src, base, n):
        weighted = mm(wsel[order], src[:, chunk(n)])
        out_ref[:, chunk(n, base)] = (hidden[:, chunk(n, base)] + weighted[0:32] + weighted[32:64]).astype(BF)

    ex_wait(3, ta2, ua2)
    loop(0, 5, lambda n: combine(0, ua2, 0, n))
    sq_wait(3, tb2, ub2)
    loop(0, 5, lambda n: combine(1, ub2, H, n))

    for c in kv_copies:
        c.wait_send()
    for i in range(3):
        z_copy(i).wait_send()
        a2_copy(i).wait_send()
        b2_copy(i).wait_send()
        loop(0, 4, lambda j: x_copy(i, j).wait_send())
    for use, src, dst in ((0, da1, ra1), (1, db2, rb2), (2, tb1, ub1), (3, ta2, ua2)):
        loop(1, 16, lambda d: ex_copy(use, src, dst, d).wait_send())
    for use, src, dst in ((0, db1, rb1), (1, da2, ra2), (2, ta1, ua1), (3, tb2, ub2)):
        loop(1, 8, lambda d: sq_copy(use, src, dst, d).wait_send())


def per_device(
    queries, key_rows, value_rows, sink_logits, out_proj, residual, norm_gain, expert_ids, gate_weights,
    w_gate_up, w_down,
):
    hbm = pl.BlockSpec(memory_space=pl.ANY)
    vmem = pl.BlockSpec(memory_space=pltpu.VMEM)
    smem = pl.BlockSpec(memory_space=pltpu.SMEM)
    dma = pltpu.SemaphoreType.DMA
    wide = pltpu.VMEM((256, H), BF)
    scratch = [
        pltpu.VMEM((512, 256), BF),
        pltpu.VMEM((32, 512), BF),
        pltpu.VMEM((32, 512), BF),
        pltpu.VMEM((256, D), BF),
        pltpu.VMEM((32, D), BF),
        pltpu.VMEM((1, 2 * FF, D), BF),
        pltpu.VMEM((1, FF, D), BF),
        pltpu.VMEM((2, 64, 640), BF),
        pltpu.VMEM((128, 512), BF),
        pltpu.VMEM((128, 512), BF),
        pltpu.VMEM((128, 256), BF),
        pltpu.VMEM((4, 128, H), BF),
        pltpu.VMEM((4, 128, H), BF),
        pltpu.VMEM((4, 128, H), BF),
        pltpu.VMEM((4, 4, 32, H), BF),
        pltpu.VMEM((128, H), BF),
        pltpu.VMEM((4, 32, H), BF),
        pltpu.VMEM((4, 32, H), BF),
        pltpu.VMEM((4, 32, H), BF),
        pltpu.VMEM((32, D), F32),
        pltpu.VMEM((32, D), BF),
        pltpu.VMEM((2, 256, 32), BF),
        pltpu.VMEM((2, 64, 256), BF),
        pltpu.VMEM((2, 256, 256), BF),
        *[wide] * 9,
        pltpu.VMEM((256, FF), BF),
        *[wide] * 9,
        dma((7,)),
        dma((3,)),
        dma((3,)),
        dma((3,)),
        dma((3,)),
        dma((3, 4)),
        dma((3, 4)),
        dma((3,)),
        dma((3,)),
        dma((3,)),
        dma((3,)),
        dma((4, 15)),
        dma((4, 15)),
        dma((4, 7)),
        dma((4, 7)),
    ]
    return pl.pallas_call(
        layer_kernel,
        out_shape=jax.ShapeDtypeStruct((32, D), BF),
        in_specs=[hbm, hbm, hbm, smem, hbm, hbm, vmem, vmem, vmem, hbm, hbm],
        out_specs=vmem,
        scratch_shapes=scratch,
        compiler_params=pltpu.CompilerParams(
            collective_id=1, has_side_effects=True, vmem_limit_bytes=60 * 1024 * 1024
        ),
        name="layer",
    )(
        queries, key_rows.T, value_rows.T, sink_logits, out_proj, residual, norm_gain,
        expert_ids.T, gate_weights.T, jnp.swapaxes(w_gate_up, 1, 2), w_down,
    )


def solution(mesh):
    return jax.shard_map(
        per_device,
        mesh=mesh,
        in_specs=(
            P("seq", "exp"),
            P("seq", "exp"),
            P("seq", "exp"),
            P("exp"),
            P("exp", None),
            P(("seq", "exp"), None),
            P(),
            P(("seq", "exp"), None),
            P(("seq", "exp"), None),
            P(("seq", "exp"), None, None),
            P(("seq", "exp"), None, None),
        ),
        out_specs=P(("seq", "exp"), None),
        check_vma=False,
    )
```

```python
import math

import jax
import jax.numpy as jnp
from jax import lax
from jax.experimental import pallas as pl
from jax.experimental.pallas import tpu as pltpu
from jax.sharding import PartitionSpec as P

MESH = pl.DeviceIdType.MESH
BF = jnp.bfloat16
F32 = jnp.float32
D = 2560
H = 1280
FF = 1440
COL = 256
CHUNKS = 5
CHUNK = 512


def mm(a, b):
    return jnp.dot(a, b, preferred_element_type=F32)


def mm_nt(a, b):
    return lax.dot_general(a, b, (((1,), (1,)), ((), ())), preferred_element_type=F32)


def remote(src, dst, send_sem, recv_sem, device):
    return pltpu.make_async_remote_copy(
        src, dst, send_sem, recv_sem, device_id=device, device_id_type=MESH
    )


def aligned(value, multiple):
    return pl.multiple_of(value, multiple)


def loop(low, high, body):
    def step(i, carry):
        body(i)
        return carry

    lax.fori_loop(low, high, step, 0)


def layer_kernel(
    q_hbm, k_hbm, v_hbm, sink_ref, wo_hbm, res_hbm, gain_ref, ids_ref, gates_ref, wgu_hbm, wd_hbm,
    out_ref,
    q, kraw, vraw, wo, res, wgu, wd,
    kext, bdk, bdv, att,
    part_a, part_b, recv_z, recv_x, sum_a, sum_b, recv_a2, recv_b2,
    hidden, metas, select, weigh,
    tokens, slots, rows_in, acc_gate, acc_lift, act, rows_out, answers, partial, returned,
    load_sem, kv_send, kv_recv, z_send, z_recv, x_send, x_recv, a2_send, a2_recv, b2_send, b2_recv,
    meta_send, meta_recv, ex_send, ex_recv, sq_send, sq_recv,
):
    s = lax.axis_index("seq")
    e = lax.axis_index("exp")
    z = e // 4
    x = lax.rem(e, 4)
    parity = lax.rem(e, 2)
    mate = e + 1 - 2 * parity
    s_next = lax.rem(s + 1, 8)
    s_last = lax.rem(s + 7, 8)

    loads = [
        pltpu.make_async_copy(a, b, load_sem.at[i])
        for i, (a, b) in enumerate(
            [(k_hbm, kraw), (v_hbm, vraw), (q_hbm, q), (wo_hbm, wo), (res_hbm, res), (wgu_hbm, wgu), (wd_hbm, wd)]
        )
    ]
    for c in loads:
        c.start()

    barrier = pltpu.get_barrier_semaphore()

    def greet(device):
        pl.semaphore_signal(barrier, inc=1, device_id=device, device_id_type=MESH)

    loop(1, 16, lambda d: greet((s, lax.rem(e + d, 16))))
    loop(1, 8, lambda d: greet((lax.rem(s + d, 8), e)))
    greet((s_next, mate))
    greet((s_last, mate))

    loads[0].wait()
    kext[parity, 0:32, 128:640] = kraw[...]
    loads[1].wait()
    kext[parity, 32:64, 128:640] = vraw[...]
    pl.semaphore_wait(barrier, 24)
    own_rows = kext.at[parity, :, pl.ds(128, 512)]
    own_tail = kext.at[parity, :, pl.ds(512, 128)]
    prior = kext.at[parity, :, pl.ds(0, 128)]
    kv_copies = [
        remote(own_rows, own_rows, kv_send.at[0], kv_recv.at[0], (s, mate)),
        remote(own_tail, prior, kv_send.at[1], kv_recv.at[1], (s_next, e)),
        remote(own_tail, prior, kv_send.at[2], kv_recv.at[2], (s_next, mate)),
    ]
    for c in kv_copies:
        c.start()

    own_lanes = (
        lax.broadcasted_iota(jnp.int32, (32, 256), 1)
        == lax.broadcasted_iota(jnp.int32, (32, 256), 0) + s * 32
    )
    own_lanes = jnp.where(own_lanes, 1.0, 0.0)
    for part, ref in ((slice(0, 4), ids_ref), (slice(4, 8), gates_ref)):
        metas[s, part, :] = jnp.dot(
            ref[...].astype(F32), own_lanes, preferred_element_type=F32, precision=lax.Precision.HIGHEST
        )

    def meta_copy(d):
        return remote(metas.at[s], metas.at[s], meta_send.at[d - 1], meta_recv.at[d - 1], (lax.rem(s + d, 8), e))

    loop(1, 8, lambda d: meta_copy(d).start())

    bdk[...] = jnp.zeros((128, 512), BF)
    bdv[...] = jnp.zeros((128, 512), BF)
    loads[2].wait()
    loads[3].wait()
    for c in kv_copies:
        c.wait_recv()

    def z_copy(i):
        b = lax.rem(z + 1 + i, 4)
        return remote(part_a.at[b], recv_z.at[z], z_send.at[i], z_recv.at[i], (s, b * 4 + x))

    def x_copy(d, i):
        b = lax.rem(z + 1 + i, 4)
        other = lax.rem(x + 1 + d, 4)
        return remote(
            part_b.at[b, pl.ds(aligned(other * 32, 32), 32)],
            recv_x.at[x, b],
            x_send.at[d, i],
            x_recv.at[d, i],
            (s, z * 4 + other),
        )

    query_pos = lax.broadcasted_iota(jnp.int32, (128, 256), 0)
    key_pos = lax.broadcasted_iota(jnp.int32, (128, 256), 1)
    inside = (key_pos > query_pos) & (key_pos <= query_pos + 128)

    def attend(i):
        b = lax.rem(z + 1 + i, 4)
        window = pl.ds(aligned(b * 128, 128), 256)
        for half in range(2):
            for p in range(2):
                rows = slice(half * 64 + p * 32, half * 64 + p * 32 + 32)
                bdk[rows, half * 256 : half * 256 + 256] = kext[p, 0:32, window]
                bdv[rows, half * 256 : half * 256 + 256] = kext[p, 32:64, window]
        allowed = inside & (key_pos + (s * 512 + b * 128) >= 128)
        for pair in range(2):
            queries = q[pl.ds(aligned(b * 128, 128), 128), pair * 128 : pair * 128 + 128]
            scores = mm(queries, bdk[...]) * (1.0 / math.sqrt(64))
            probs = []
            for half in range(2):
                sink = sink_ref[pair * 2 + half]
                part = jnp.where(allowed, scores[:, half * 256 : half * 256 + 256], -1e30)
                highest = jnp.maximum(jnp.max(part, axis=1, keepdims=True), sink)
                raised = jnp.exp(part - highest)
                total = jnp.sum(raised, axis=1, keepdims=True) + jnp.exp(sink - highest)
                probs.append((raised * (1.0 / total)).astype(BF))
            mixed = mm_nt(jnp.concatenate(probs, axis=1), bdv[...])
            att[:, pair * 128 : pair * 128 + 128] = mixed.astype(BF)
        attended = att[...]
        for n in range(5):
            part_a[b, :, n * COL : n * COL + COL] = mm(attended, wo[:, n * COL : n * COL + COL]).astype(BF)

        @pl.when(i < 3)
        def _():
            z_copy(i).start()

        for n in range(5):
            part_b[b, :, n * COL : n * COL + COL] = mm(
                attended, wo[:, H + n * COL : H + n * COL + COL]
            ).astype(BF)
        for d in range(3):
            x_copy(d, i).start()

    loop(0, 4, attend)

    loop(1, 8, lambda d: meta_copy(d).wait_recv())
    meta = metas[0]
    for i in range(1, 8):
        meta = meta + metas[i]
    place = lax.broadcasted_iota(jnp.int32, (256, 256), 0)
    token = lax.broadcasted_iota(jnp.int32, (256, 256), 1)
    mine = ((place & 15) >> 1) == (token >> 5)
    expert = ((place >> 4) + s * 16).astype(F32)
    named = jnp.zeros((256, 256), F32)
    weight = jnp.zeros((256, 256), F32)
    for k in range(4):
        same = mine & (meta[k : k + 1, :] == expert)
        named = named + jnp.where(same, 1.0, 0.0)
        weight = weight + jnp.where(same, meta[4 + k : 5 + k, :], 0.0)
    before = jnp.where(place < token, 1.0, 0.0).astype(BF)
    rank = mm(named.astype(BF), before)
    chosen = jnp.where(rank == (place & 1).astype(F32), named, 0.0)
    select[...] = chosen.astype(BF)
    weight = jnp.transpose(weight * chosen)
    high = weight.astype(BF)
    weigh[0] = high
    weigh[1] = (weight - high.astype(F32)).astype(BF)

    def a2_copy(i):
        other = lax.rem(x + 1 + i, 4)
        return remote(
            sum_a.at[pl.ds(aligned(other * 32, 32), 32)],
            recv_a2.at[x],
            a2_send.at[i],
            a2_recv.at[i],
            (s, z * 4 + other),
        )

    def b2_copy(i):
        b = lax.rem(z + 1 + i, 4)
        return remote(sum_b.at[b], recv_b2.at[z], b2_send.at[i], b2_recv.at[i], (s, b * 4 + x))

    for i in range(3):
        z_copy(i).wait_recv()

    def sum_over_z(i):
        other = lax.rem(x + 1 + i, 4)
        rows = pl.ds(aligned(other * 32, 32), 32)
        total = part_a[z, rows, :].astype(F32)
        for d in range(1, 4):
            total = total + recv_z[lax.rem(z + d, 4), rows, :].astype(F32)
        sum_a[rows, :] = total.astype(BF)

        @pl.when(i < 3)
        def _():
            a2_copy(i).start()

    loop(0, 4, sum_over_z)

    def sum_over_x(i):
        b = lax.rem(z + 1 + i, 4)
        for d in range(3):
            x_copy(d, i).wait_recv()
        total = part_b[b, pl.ds(aligned(x * 32, 32), 32), :].astype(F32)
        for d in range(1, 4):
            total = total + recv_x[lax.rem(x + d, 4), b].astype(F32)
        sum_b[b] = total.astype(BF)

        @pl.when(i < 3)
        def _():
            b2_copy(i).start()

    loop(0, 4, sum_over_x)

    loads[4].wait()
    for i in range(3):
        a2_copy(i).wait_recv()
    total = sum_a[pl.ds(aligned(x * 32, 32), 32), :].astype(F32)
    for d in range(1, 4):
        total = total + recv_a2[lax.rem(x + d, 4)].astype(F32)
    hidden_a = res[:, 0:H].astype(F32) + total
    hidden[:, 0:H] = hidden_a
    for i in range(3):
        b2_copy(i).wait_recv()
    total = sum_b[z].astype(F32)
    for d in range(1, 4):
        total = total + recv_b2[lax.rem(z + d, 4)].astype(F32)
    hidden_b = res[:, H:D].astype(F32) + total
    hidden[:, H:D] = hidden_b
    squares = jnp.sum(hidden_a * hidden_a, axis=1, keepdims=True) + jnp.sum(
        hidden_b * hidden_b, axis=1, keepdims=True
    )
    scale = lax.rsqrt(squares * (1.0 / D) + 1e-05)
    gain = gain_ref[...].reshape(1, D)

    own_block = pl.ds(aligned(s * 32, 32), 32)
    own_slots = pl.ds(aligned(e * 16, 16), 16)

    def sq_copy(use, c, d):
        peer = lax.rem(s + d, 8)
        src, dst, rows = (tokens, tokens, own_block)
        if use == 1:
            src, dst, rows = (partial, returned, pl.ds(aligned(peer * 32, 32), 32))
        return remote(
            src.at[c, rows], dst.at[c, own_block], sq_send.at[use, c, d - 1], sq_recv.at[use, c, d - 1], (peer, e)
        )

    def ex_copy(use, c, d):
        peer = lax.rem(e + d, 16)
        src, dst = (slots, rows_in) if use == 0 else (rows_out, answers)
        return remote(
            src.at[c, pl.ds(aligned(peer * 16, 16), 16)],
            dst.at[c, own_slots],
            ex_send.at[use, c, d - 1],
            ex_recv.at[use, c, d - 1],
            (s, peer),
        )

    def columns(c):
        return slice(c * CHUNK, c * CHUNK + CHUNK)

    for c in range(CHUNKS):
        tokens[c, own_block, :] = (hidden[:, columns(c)] * scale * gain[:, columns(c)]).astype(BF)
        loop(1, 8, lambda d: sq_copy(0, c, d).start())

    def dispatch(c):
        loop(1, 8, lambda d: sq_copy(0, c, d).wait_recv())
        for n in (slice(0, COL), slice(COL, CHUNK)):
            slots[c, :, n] = mm(select[...], tokens[c, :, n]).astype(BF)
        loop(1, 16, lambda d: ex_copy(0, c, d).start())
        rows_in[c, own_slots, :] = slots[c, own_slots, :]

    def up_tile(c, low, width):
        out = pl.ds(aligned(low, 128), width)
        tiles = []
        for base, acc in ((0, acc_gate), (FF, acc_lift)):
            weights = wgu[0, pl.ds(aligned(base + low, 16), width), columns(c)]
            tile = mm_nt(rows_in[c], weights)
            if c > 0:
                tile = tile + acc[:, out]
            if c < CHUNKS - 1:
                acc[:, out] = tile
            tiles.append(tile)
        if c == CHUNKS - 1:
            gate, lift = tiles
            act[:, out] = (gate * (1.0 / (1.0 + jnp.exp(-1.702 * gate))) * (lift + 1.0)).astype(BF)

    def up(c):
        loop(1, 16, lambda d: ex_copy(0, c, d).wait_recv())
        loop(0, 5, lambda n: up_tile(c, n * COL, COL))
        up_tile(c, 5 * COL, FF - 5 * COL)

    dispatch(0)
    dispatch(1)
    loads[5].wait()
    for c in range(CHUNKS):
        up(c)
        if c + 2 < CHUNKS:
            dispatch(c + 2)

    loads[6].wait()
    for c in range(CHUNKS):
        for n in range(2):
            low = c * CHUNK + n * COL
            rows_out[c, :, n * COL : n * COL + COL] = mm(act[...], wd[0, :, low : low + COL]).astype(BF)
        loop(1, 16, lambda d: ex_copy(1, c, d).start())
        answers[c, own_slots, :] = rows_out[c, own_slots, :]

    def combine(c):
        loop(1, 16, lambda d: ex_copy(1, c, d).wait_recv())
        for n in (slice(0, COL), slice(COL, CHUNK)):
            partial[c, :, n] = (mm(weigh[0], answers[c, :, n]) + mm(weigh[1], answers[c, :, n])).astype(BF)
        loop(1, 8, lambda d: sq_copy(1, c, d).start())
        returned[c, own_block, :] = partial[c, own_block, :]

    def finish(c):
        loop(1, 8, lambda d: sq_copy(1, c, d).wait_recv())
        total = hidden[:, columns(c)]
        for i in range(8):
            total = total + returned[c, i * 32 : i * 32 + 32, :].astype(F32)
        out_ref[:, columns(c)] = total.astype(BF)

    combine(0)
    combine(1)
    for c in range(CHUNKS):
        if c + 2 < CHUNKS:
            combine(c + 2)
        finish(c)

    for c in kv_copies:
        c.wait_send()
    for i in range(3):
        z_copy(i).wait_send()
        a2_copy(i).wait_send()
        b2_copy(i).wait_send()
        loop(0, 4, lambda j: x_copy(i, j).wait_send())
    loop(1, 8, lambda d: meta_copy(d).wait_send())
    for use in range(2):
        for c in range(CHUNKS):
            loop(1, 16, lambda d: ex_copy(use, c, d).wait_send())
            loop(1, 8, lambda d: sq_copy(use, c, d).wait_send())


def per_device(
    queries, key_rows, value_rows, sink_logits, out_proj, residual, norm_gain, expert_ids, gate_weights,
    w_gate_up, w_down,
):
    hbm = pl.BlockSpec(memory_space=pl.ANY)
    vmem = pl.BlockSpec(memory_space=pltpu.VMEM)
    smem = pl.BlockSpec(memory_space=pltpu.SMEM)
    dma = pltpu.SemaphoreType.DMA
    wide = pltpu.VMEM((CHUNKS, 256, CHUNK), BF)
    scratch = [
        pltpu.VMEM((512, 256), BF),
        pltpu.VMEM((32, 512), BF),
        pltpu.VMEM((32, 512), BF),
        pltpu.VMEM((256, D), BF),
        pltpu.VMEM((32, D), BF),
        pltpu.VMEM((1, 2 * FF, D), BF),
        pltpu.VMEM((1, FF, D), BF),
        pltpu.VMEM((2, 64, 640), BF),
        pltpu.VMEM((128, 512), BF),
        pltpu.VMEM((128, 512), BF),
        pltpu.VMEM((128, 256), BF),
        pltpu.VMEM((4, 128, H), BF),
        pltpu.VMEM((4, 128, H), BF),
        pltpu.VMEM((4, 128, H), BF),
        pltpu.VMEM((4, 4, 32, H), BF),
        pltpu.VMEM((128, H), BF),
        pltpu.VMEM((4, 32, H), BF),
        pltpu.VMEM((4, 32, H), BF),
        pltpu.VMEM((4, 32, H), BF),
        pltpu.VMEM((32, D), F32),
        pltpu.VMEM((8, 8, 256), F32),
        pltpu.VMEM((256, 256), BF),
        pltpu.VMEM((2, 256, 256), BF),
        wide,
        wide,
        wide,
        pltpu.VMEM((256, FF), F32),
        pltpu.VMEM((256, FF), F32),
        pltpu.VMEM((256, FF), BF),
        wide,
        wide,
        wide,
        wide,
        dma((7,)),
        dma((3,)),
        dma((3,)),
        dma((3,)),
        dma((3,)),
        dma((3, 4)),
        dma((3, 4)),
        dma((3,)),
        dma((3,)),
        dma((3,)),
        dma((3,)),
        dma((7,)),
        dma((7,)),
        dma((2, CHUNKS, 15)),
        dma((2, CHUNKS, 15)),
        dma((2, CHUNKS, 7)),
        dma((2, CHUNKS, 7)),
    ]
    return pl.pallas_call(
        layer_kernel,
        out_shape=jax.ShapeDtypeStruct((32, D), BF),
        in_specs=[hbm, hbm, hbm, smem, hbm, hbm, vmem, vmem, vmem, hbm, hbm],
        out_specs=vmem,
        scratch_shapes=scratch,
        compiler_params=pltpu.CompilerParams(
            collective_id=1, has_side_effects=True, vmem_limit_bytes=60 * 1024 * 1024
        ),
        name="layer",
    )(
        queries, key_rows.T, value_rows.T, sink_logits, out_proj, residual, norm_gain,
        expert_ids.T, gate_weights.T, jnp.swapaxes(w_gate_up, 1, 2), w_down,
    )


def solution(mesh):
    return jax.shard_map(
        per_device,
        mesh=mesh,
        in_specs=(
            P("seq", "exp"),
            P("seq", "exp"),
            P("seq", "exp"),
            P("exp"),
            P("exp", None),
            P(("seq", "exp"), None),
            P(),
            P(("seq", "exp"), None),
            P(("seq", "exp"), None),
            P(("seq", "exp"), None, None),
            P(("seq", "exp"), None, None),
        ),
        out_specs=P(("seq", "exp"), None),
        check_vma=False,
    )
```

```python
import math

import jax
import jax.numpy as jnp
from jax import lax
from jax.experimental import pallas as pl
from jax.experimental.pallas import tpu as pltpu
from jax.sharding import PartitionSpec as P

MESH = pl.DeviceIdType.MESH
BF = jnp.bfloat16
F32 = jnp.float32
D = 2560
FF = 1440
COL = 256
CHUNKS = 5
CHUNK = 512
EXTRA = 128


def mm(a, b):
    return jnp.dot(a, b, preferred_element_type=F32)


def mm_nt(a, b):
    return lax.dot_general(a, b, (((1,), (1,)), ((), ())), preferred_element_type=F32)


def remote(src, dst, send_sem, recv_sem, device):
    return pltpu.make_async_remote_copy(
        src, dst, send_sem, recv_sem, device_id=device, device_id_type=MESH
    )


def aligned(value, multiple):
    return pl.multiple_of(value, multiple)


def loop(low, high, body):
    def step(i, carry):
        body(i)
        return carry

    lax.fori_loop(low, high, step, 0)


def layer_kernel(
    q_hbm, k_hbm, v_hbm, sink_ref, wo_hbm, res_hbm, gain_ref, ids_ref, gates_ref, wgu_hbm, wd_hbm,
    out_ref,
    q, kraw, vraw, wo, res, wgu, wd,
    kext, bdk, bdv, att,
    shares, recv_z, recv_x, sum_a, sum_b, recv_a2, recv_b2,
    hidden, metas, select, weigh,
    tokens_first, tokens_last, slots_first, slots_last, rows_first, rows_last,
    acc_gate, acc_lift, act, rows_out, answers, partial, crossed, summed, returned,
    load_sem, kv_send, kv_recv, first_send, first_recv, second_send, second_recv,
    meta_send, meta_recv, ex_send, ex_recv, gather_send, gather_recv, relay_send, relay_recv, cross_send, cross_recv,
    home_send, home_recv,
):
    s = lax.axis_index("seq")
    e = lax.axis_index("exp")
    z = e // 4
    x = lax.rem(e, 4)
    parity = lax.rem(e, 2)
    mate = e + 1 - 2 * parity
    y = s // 2
    core = lax.rem(s, 2)
    twin = s + 1 - 2 * core
    s_next = lax.rem(s + 1, 8)
    s_last = lax.rem(s + 7, 8)

    loads = [
        pltpu.make_async_copy(a, b, load_sem.at[i])
        for i, (a, b) in enumerate(
            [(k_hbm, kraw), (v_hbm, vraw), (q_hbm, q), (wo_hbm, wo), (res_hbm, res), (wgu_hbm, wgu), (wd_hbm, wd)]
        )
    ]
    for c in loads:
        c.start()

    barrier = pltpu.get_barrier_semaphore()

    def greet(device):
        pl.semaphore_signal(barrier, inc=1, device_id=device, device_id_type=MESH)

    loop(1, 16, lambda d: greet((s, lax.rem(e + d, 16))))
    loop(1, 8, lambda d: greet((lax.rem(s + d, 8), e)))
    greet((s_next, mate))
    greet((s_last, mate))

    loads[0].wait()
    kext[parity, 0:32, 128:640] = kraw[...]
    loads[1].wait()
    kext[parity, 32:64, 128:640] = vraw[...]
    pl.semaphore_wait(barrier, 24)
    own_rows = kext.at[parity, :, pl.ds(128, 512)]
    own_tail = kext.at[parity, :, pl.ds(512, 128)]
    prior = kext.at[parity, :, pl.ds(0, 128)]
    kv_copies = [
        remote(own_rows, own_rows, kv_send.at[0], kv_recv.at[0], (s, mate)),
        remote(own_tail, prior, kv_send.at[1], kv_recv.at[1], (s_next, e)),
        remote(own_tail, prior, kv_send.at[2], kv_recv.at[2], (s_next, mate)),
    ]
    for c in kv_copies:
        c.start()

    own_lanes = (
        lax.broadcasted_iota(jnp.int32, (32, 256), 1)
        == lax.broadcasted_iota(jnp.int32, (32, 256), 0) + s * 32
    )
    own_lanes = jnp.where(own_lanes, 1.0, 0.0)
    for part, ref in ((slice(0, 4), ids_ref), (slice(4, 8), gates_ref)):
        metas[s, part, :] = jnp.dot(
            ref[...].astype(F32), own_lanes, preferred_element_type=F32, precision=lax.Precision.HIGHEST
        )

    def meta_copy(d):
        return remote(metas.at[s], metas.at[s], meta_send.at[d - 1], meta_recv.at[d - 1], (lax.rem(s + d, 8), e))

    loop(1, 8, lambda d: meta_copy(d).start())

    bdk[...] = jnp.zeros((128, 512), BF)
    bdv[...] = jnp.zeros((128, 512), BF)
    loads[2].wait()
    loads[3].wait()
    for c in kv_copies:
        c.wait_recv()

    query_pos = lax.broadcasted_iota(jnp.int32, (128, 256), 0)
    key_pos = lax.broadcasted_iota(jnp.int32, (128, 256), 1)
    inside = (key_pos > query_pos) & (key_pos <= query_pos + 128)

    def attend(b):
        window = pl.ds(aligned(b * 128, 128), 256)
        for half in range(2):
            for p in range(2):
                rows = slice(half * 64 + p * 32, half * 64 + p * 32 + 32)
                bdk[rows, half * 256 : half * 256 + 256] = kext[p, 0:32, window]
                bdv[rows, half * 256 : half * 256 + 256] = kext[p, 32:64, window]
        allowed = inside & (key_pos + (s * 512 + b * 128) >= 128)
        for pair in range(2):
            queries = q[pl.ds(aligned(b * 128, 128), 128), pair * 128 : pair * 128 + 128]
            scores = mm(queries, bdk[...]) * (1.0 / math.sqrt(64))
            probs = []
            for half in range(2):
                sink = sink_ref[pair * 2 + half]
                part = jnp.where(allowed, scores[:, half * 256 : half * 256 + 256], -1e30)
                highest = jnp.maximum(jnp.max(part, axis=1, keepdims=True), sink)
                raised = jnp.exp(part - highest)
                total = jnp.sum(raised, axis=1, keepdims=True) + jnp.exp(sink - highest)
                probs.append((raised * (1.0 / total)).astype(BF))
            mixed = mm_nt(jnp.concatenate(probs, axis=1), bdv[...])
            att[pl.ds(aligned(b * 128, 128), 128), pair * 128 : pair * 128 + 128] = mixed.astype(BF)

    loop(0, 4, attend)

    def columns(c):
        return slice(c * CHUNK, c * CHUNK + CHUNK)

    def project(c):
        for half in range(2):
            low = c * CHUNK + half * COL
            shares[c, half] = mm(att[...], wo[:, low : low + COL]).reshape(4, 128, COL).astype(BF)
            for i in range(3):
                first_copy(c, half, i).start()

    def z_peer(i):
        return lax.rem(z + 1 + i, 4)

    def x_peer(i):
        return lax.rem(x + 1 + i, 4)

    def rows_of(peer):
        return pl.ds(aligned(peer * 32, 32), 32)

    def first_copy(c, half, i):
        if half == 0:
            src, dst, peer = shares.at[c, 0, z_peer(i)], recv_z.at[c, z], z_peer(i) * 4 + x
        else:
            src, dst, peer = shares.at[c, 1, :, rows_of(x_peer(i))], recv_x.at[c, x], z * 4 + x_peer(i)
        return remote(src, dst, first_send.at[c, half, i], first_recv.at[c, half, i], (s, peer))

    def second_copy(c, half, i):
        if half == 0:
            src, dst, peer = sum_a.at[c, rows_of(x_peer(i))], recv_a2.at[c, x], z * 4 + x_peer(i)
        else:
            src, dst, peer = sum_b.at[c, z_peer(i)], recv_b2.at[c, z], z_peer(i) * 4 + x
        return remote(src, dst, second_send.at[c, half, i], second_recv.at[c, half, i], (s, peer))

    def sum_first(c):
        for i in range(3):
            first_copy(c, 0, i).wait_recv()
        total = shares[c, 0, z].astype(F32)
        for i in range(3):
            total = total + recv_z[c, z_peer(i)].astype(F32)
        sum_a[c] = total.astype(BF)
        for i in range(3):
            second_copy(c, 0, i).start()
        for i in range(3):
            first_copy(c, 1, i).wait_recv()
        total = shares[c, 1, :, rows_of(x), :].astype(F32)
        for i in range(3):
            total = total + recv_x[c, x_peer(i)].astype(F32)
        sum_b[c] = total.astype(BF)
        for i in range(3):
            second_copy(c, 1, i).start()

    own_block = pl.ds(aligned(s * 32, 32), 32)
    own_slots = pl.ds(aligned(e * 16, 16), 16)

    def along_y(k):
        return lax.rem(y + k, 4) * 2 + core

    def gather_copy(c, k):
        block = tokens(c).at[own_block]
        peer = twin if k == 0 else along_y(k)
        return remote(block, block, gather_send.at[c, k], gather_recv.at[c, k], (peer, e))

    def relay_copy(c, k):
        block = tokens(c).at[pl.ds(aligned(along_y(4 - k) * 32, 32), 32)]
        return remote(block, block, relay_send.at[c, k - 1], relay_recv.at[c, k - 1], (twin, e))

    def cross_copy(c):
        return remote(partial.at[c, :, 1 - core], crossed.at[c], cross_send.at[c], cross_recv.at[c], (twin, e))

    def home_copy(c, k):
        return remote(
            summed.at[c, lax.rem(y + k, 4)],
            returned.at[c, y],
            home_send.at[c, k - 1],
            home_recv.at[c, k - 1],
            (along_y(k), e),
        )

    def tokens(c):
        return tokens_last if c == CHUNKS - 1 else tokens_first.at[c]

    def slots(c):
        return slots_last if c == CHUNKS - 1 else slots_first.at[c]

    def rows_in(c):
        return rows_last if c == CHUNKS - 1 else rows_first.at[c]

    squares = []

    def sum_second(c):
        for half, sums, place, received, peers in (
            (0, sum_a, rows_of(x), recv_a2, x_peer),
            (1, sum_b, z, recv_b2, z_peer),
        ):
            for i in range(3):
                second_copy(c, half, i).wait_recv()
            low = c * CHUNK + half * COL
            total = res[:, low : low + COL].astype(F32) + sums[c, place].astype(F32)
            for i in range(3):
                total = total + received[c, peers(i)].astype(F32)
            hidden[:, low : low + COL] = total
            squares.append(jnp.sum(total * total, axis=1, keepdims=True))
            tokens(c)[own_block, half * COL : half * COL + COL] = (total * gain[:, low : low + COL]).astype(BF)
        if c == CHUNKS - 1:
            mean = sum(squares[1:], squares[0]) * (1.0 / D)
            rest = jnp.broadcast_to(lax.rsqrt(mean + 1e-05), (32, EXTRA))
            lane = lax.broadcasted_iota(jnp.int32, (32, EXTRA), 1)
            parts = jnp.zeros((32, EXTRA), F32)
            for i in range(3):
                rounded = rest.astype(BF).astype(F32)
                parts = jnp.where(lane == i, rounded, parts)
                rest = rest - rounded
            tokens(c)[own_block, CHUNK : CHUNK + EXTRA] = parts.astype(BF)
        for k in (1, 3, 2, 0):
            gather_copy(c, k).start()

    def ex_copy(use, c, d):
        peer = lax.rem(e + d, 16)
        src, dst = (slots(c), rows_in(c)) if use == 0 else (rows_out.at[c], answers.at[c])
        return remote(
            src.at[pl.ds(aligned(peer * 16, 16), 16)],
            dst.at[own_slots],
            ex_send.at[use, c, d - 1],
            ex_recv.at[use, c, d - 1],
            (s, peer),
        )

    def relay(c):
        for k in (1, 3, 2):
            gather_copy(c, k).wait_recv()
            relay_copy(c, k).start()

    def dispatch(c):
        gather_copy(c, 0).wait_recv()
        for k in (1, 3, 2):
            relay_copy(c, k).wait_recv()
        pieces = [slice(0, COL), slice(COL, CHUNK)]
        if c == CHUNKS - 1:
            pieces.append(slice(CHUNK, CHUNK + EXTRA))
        for n in pieces:
            slots(c)[:, n] = mm(select[...], tokens(c)[:, n]).astype(BF)
        loop(1, 16, lambda d: ex_copy(0, c, d).start())
        rows_in(c)[own_slots, :] = slots(c)[own_slots, :]

    def up_tile(c, low, width, scale):
        out = pl.ds(aligned(low, 128), width)
        tiles = []
        for base, acc in ((0, acc_gate), (FF, acc_lift)):
            weights = wgu[0, pl.ds(aligned(base + low, 16), width), columns(c)]
            tile = mm_nt(rows_in(c)[:, 0:CHUNK], weights)
            if c > 0:
                tile = tile + acc[:, out]
            if c < CHUNKS - 1:
                acc[:, out] = tile
            tiles.append(tile)
        if c == CHUNKS - 1:
            gate, lift = tiles[0] * scale, tiles[1] * scale
            act[:, out] = (gate * (1.0 / (1.0 + jnp.exp(-1.702 * gate))) * (lift + 1.0)).astype(BF)

    def up(c):
        loop(1, 16, lambda d: ex_copy(0, c, d).wait_recv())
        scale = None
        if c == CHUNKS - 1:
            scale = jnp.sum(rows_in(c)[:, CHUNK : CHUNK + EXTRA].astype(F32), axis=1, keepdims=True)
        for n in range(5):
            up_tile(c, n * COL, COL, scale)
        up_tile(c, 5 * COL, FF - 5 * COL, scale)

    project(0)
    project(1)
    loop(1, 8, lambda d: meta_copy(d).wait_recv())
    meta = metas[0]
    for i in range(1, 8):
        meta = meta + metas[i]
    place = lax.broadcasted_iota(jnp.int32, (256, 256), 0)
    token = lax.broadcasted_iota(jnp.int32, (256, 256), 1)
    mine = ((place & 15) >> 1) == (token >> 5)
    expert = ((place >> 4) + s * 16).astype(F32)
    named = jnp.zeros((256, 256), F32)
    weight = jnp.zeros((256, 256), F32)
    for k in range(4):
        same = mine & (meta[k : k + 1, :] == expert)
        named = named + jnp.where(same, 1.0, 0.0)
        weight = weight + jnp.where(same, meta[4 + k : 5 + k, :], 0.0)
    before = jnp.where(place < token, 1.0, 0.0).astype(BF)
    rank = mm(named.astype(BF), before)
    chosen = jnp.where(rank == (place & 1).astype(F32), named, 0.0)
    select[...] = chosen.astype(BF)
    weight = jnp.transpose(weight * chosen)
    high = weight.astype(BF)
    weigh[0] = high
    weigh[1] = (weight - high.astype(F32)).astype(BF)

    loads[4].wait()
    gain = gain_ref[...].reshape(1, D)
    for step in range(CHUNKS + 3):
        if step < CHUNKS:
            sum_first(step)
        if step + 2 < CHUNKS:
            project(step + 2)
        if 0 <= step - 1 < CHUNKS:
            sum_second(step - 1)
        if 0 <= step - 2 < CHUNKS:
            relay(step - 2)
        if 0 <= step - 3 < CHUNKS:
            dispatch(step - 3)
        if step == CHUNKS + 1:
            loads[5].wait()
            up(0)
    for c in range(1, CHUNKS):
        up(c)

    loads[6].wait()
    for c in range(CHUNKS):
        for n in range(2):
            low = c * CHUNK + n * COL
            rows_out[c, :, n * COL : n * COL + COL] = mm(act[...], wd[0, :, low : low + COL]).astype(BF)
        loop(1, 16, lambda d: ex_copy(1, c, d).start())
        answers[c, own_slots, :] = rows_out[c, own_slots, :]

    def combine(c):
        loop(1, 16, lambda d: ex_copy(1, c, d).wait_recv())
        for n in (slice(0, COL), slice(COL, CHUNK)):
            sums = mm(weigh[0], answers[c, :, n]) + mm(weigh[1], answers[c, :, n])
            partial[c, :, :, :, n] = sums.reshape(4, 2, 32, COL).astype(BF)
        cross_copy(c).start()

    def reduce(c):
        cross_copy(c).wait_recv()
        for i in range(4):
            summed[c, i] = (partial[c, i, core].astype(F32) + crossed[c, i].astype(F32)).astype(BF)
        for k in (1, 3, 2):
            home_copy(c, k).start()

    def finish(c):
        total = hidden[:, columns(c)] + summed[c, y].astype(F32)
        for k in range(1, 4):
            home_copy(c, k).wait_recv()
        for k in range(1, 4):
            total = total + returned[c, lax.rem(y + k, 4)].astype(F32)
        out_ref[:, columns(c)] = total.astype(BF)

    for c in kv_copies:
        c.wait_send()
    loop(1, 8, lambda d: meta_copy(d).wait_send())
    for c in range(CHUNKS):
        for half in range(2):
            for i in range(3):
                first_copy(c, half, i).wait_send()
                second_copy(c, half, i).wait_send()
        for k in range(4):
            gather_copy(c, k).wait_send()
        for k in range(1, 4):
            relay_copy(c, k).wait_send()
        loop(1, 16, lambda d: ex_copy(0, c, d).wait_send())

    combine(0)
    for c in range(1, CHUNKS):
        reduce(c - 1)
        combine(c)
    reduce(CHUNKS - 1)
    for c in range(CHUNKS):
        loop(1, 16, lambda d: ex_copy(1, c, d).wait_send())
        finish(c)

    for c in range(CHUNKS):
        cross_copy(c).wait_send()
        for k in range(1, 4):
            home_copy(c, k).wait_send()


def per_device(
    queries, key_rows, value_rows, sink_logits, out_proj, residual, norm_gain, expert_ids, gate_weights,
    w_gate_up, w_down,
):
    hbm = pl.BlockSpec(memory_space=pl.ANY)
    vmem = pl.BlockSpec(memory_space=pltpu.VMEM)
    smem = pl.BlockSpec(memory_space=pltpu.SMEM)
    dma = pltpu.SemaphoreType.DMA
    wide = pltpu.VMEM((CHUNKS, 256, CHUNK), BF)
    narrow = pltpu.VMEM((CHUNKS, 4, 32, CHUNK), BF)
    scratch = [
        pltpu.VMEM((512, 256), BF),
        pltpu.VMEM((32, 512), BF),
        pltpu.VMEM((32, 512), BF),
        pltpu.VMEM((256, D), BF),
        pltpu.VMEM((32, D), BF),
        pltpu.VMEM((1, 2 * FF, D), BF),
        pltpu.VMEM((1, FF, D), BF),
        pltpu.VMEM((2, 64, 640), BF),
        pltpu.VMEM((128, 512), BF),
        pltpu.VMEM((128, 512), BF),
        pltpu.VMEM((512, 256), BF),
        pltpu.VMEM((CHUNKS, 2, 4, 128, COL), BF),
        pltpu.VMEM((CHUNKS, 4, 128, COL), BF),
        pltpu.VMEM((CHUNKS, 4, 4, 32, COL), BF),
        pltpu.VMEM((CHUNKS, 128, COL), BF),
        pltpu.VMEM((CHUNKS, 4, 32, COL), BF),
        pltpu.VMEM((CHUNKS, 4, 32, COL), BF),
        pltpu.VMEM((CHUNKS, 4, 32, COL), BF),
        pltpu.VMEM((32, D), F32),
        pltpu.VMEM((8, 8, 256), F32),
        pltpu.VMEM((256, 256), BF),
        pltpu.VMEM((2, 256, 256), BF),
        *[pltpu.VMEM((CHUNKS - 1, 256, CHUNK), BF), pltpu.VMEM((256, CHUNK + EXTRA), BF)] * 3,
        pltpu.VMEM((256, FF), F32),
        pltpu.VMEM((256, FF), F32),
        pltpu.VMEM((256, FF), BF),
        wide,
        wide,
        pltpu.VMEM((CHUNKS, 4, 2, 32, CHUNK), BF),
        narrow,
        narrow,
        narrow,
        dma((7,)),
        dma((3,)),
        dma((3,)),
        *[dma((CHUNKS, 2, 3))] * 4,
        dma((7,)),
        dma((7,)),
        dma((2, CHUNKS, 15)),
        dma((2, CHUNKS, 15)),
        dma((CHUNKS, 4)),
        dma((CHUNKS, 4)),
        dma((CHUNKS, 3)),
        dma((CHUNKS, 3)),
        dma((CHUNKS,)),
        dma((CHUNKS,)),
        dma((CHUNKS, 3)),
        dma((CHUNKS, 3)),
    ]
    return pl.pallas_call(
        layer_kernel,
        out_shape=jax.ShapeDtypeStruct((32, D), BF),
        in_specs=[hbm, hbm, hbm, smem, hbm, hbm, vmem, vmem, vmem, hbm, hbm],
        out_specs=vmem,
        scratch_shapes=scratch,
        compiler_params=pltpu.CompilerParams(
            collective_id=1, has_side_effects=True, vmem_limit_bytes=60 * 1024 * 1024
        ),
        name="layer",
    )(
        queries, key_rows.T, value_rows.T, sink_logits, out_proj, residual, norm_gain,
        expert_ids.T, gate_weights.T, jnp.swapaxes(w_gate_up, 1, 2), w_down,
    )


def solution(mesh):
    return jax.shard_map(
        per_device,
        mesh=mesh,
        in_specs=(
            P("seq", "exp"),
            P("seq", "exp"),
            P("seq", "exp"),
            P("exp"),
            P("exp", None),
            P(("seq", "exp"), None),
            P(),
            P(("seq", "exp"), None),
            P(("seq", "exp"), None),
            P(("seq", "exp"), None, None),
            P(("seq", "exp"), None, None),
        ),
        out_specs=P(("seq", "exp"), None),
        check_vma=False,
    )
```

```python
import math

import jax
import jax.numpy as jnp
from jax import lax
from jax.experimental import pallas as pl
from jax.experimental.pallas import tpu as pltpu
from jax.sharding import PartitionSpec as P

MESH = pl.DeviceIdType.MESH
BF = jnp.bfloat16
F32 = jnp.float32
D = 2560
FF = 1440
COL = 256
EXTRA = 128
WIDTHS = (512, 512, 768, 512, 256)
BACK = (256, 768, 768, 512, 256)
CHUNKS = len(WIDTHS)


def mm(a, b):
    return jnp.dot(a, b, preferred_element_type=F32)


def mm_nt(a, b):
    return lax.dot_general(a, b, (((1,), (1,)), ((), ())), preferred_element_type=F32)


def remote(src, dst, send_sem, recv_sem, device):
    return pltpu.make_async_remote_copy(
        src, dst, send_sem, recv_sem, device_id=device, device_id_type=MESH
    )


def aligned(value, multiple):
    return pl.multiple_of(value, multiple)


def arrived(parts, sem):
    pltpu.make_async_copy(parts, parts, sem).wait()


def loop(low, high, body):
    def step(i, carry):
        body(i)
        return carry

    lax.fori_loop(low, high, step, 0)


def layer_kernel(
    q_hbm, k_hbm, v_hbm, sink_ref, wo_hbm, res_hbm, gain_hbm, ids_hbm, gates_hbm, wgu_hbm, wd_hbm, out_ref, *scratch
):
    take = iter(scratch)

    def per_chunk():
        return [next(take) for _ in range(CHUNKS)]

    q, kraw, vraw, wo, res, wgu, wd, gain_ref, ids_ref, gates_ref = [next(take) for _ in range(10)]
    kext, bdk, bdv, att, hidden, metas, select, weigh, acc_gate, acc_lift, act = [next(take) for _ in range(11)]
    shares, recv_z, recv_x, sum_a, sum_b, recv_a2, recv_b2 = [per_chunk() for _ in range(7)]
    tokens, slots, rows_in = [per_chunk() for _ in range(3)]
    rows_out, answers, partial, crossed, summed, returned = [per_chunk() for _ in range(6)]
    load_sem, kv_send, kv_recv, first_send, first_recv, second_send, second_recv = [next(take) for _ in range(7)]
    meta_send, meta_recv, ex_send, ex_recv, gather_send, gather_recv = [next(take) for _ in range(6)]
    relay_send, relay_recv, cross_send, cross_recv, home_send, home_recv = [next(take) for _ in range(6)]
    s = lax.axis_index("seq")
    e = lax.axis_index("exp")
    z = e // 4
    x = lax.rem(e, 4)
    parity = lax.rem(e, 2)
    mate = e + 1 - 2 * parity
    y = s // 2
    core = lax.rem(s, 2)
    twin = s + 1 - 2 * core
    s_next = lax.rem(s + 1, 8)
    s_last = lax.rem(s + 7, 8)

    loads = [
        pltpu.make_async_copy(a, b, load_sem.at[i])
        for i, (a, b) in enumerate(
            [
                (k_hbm, kraw), (v_hbm, vraw), (q_hbm, q), (wo_hbm, wo), (res_hbm, res), (wgu_hbm, wgu), (wd_hbm, wd),
                (gain_hbm, gain_ref), (ids_hbm, ids_ref), (gates_hbm, gates_ref),
            ]
        )
    ]
    for i in (0, 1, 8, 9, 2, 3, 7, 4, 5, 6):
        loads[i].start()

    barrier = pltpu.get_barrier_semaphore()

    def greet(device):
        pl.semaphore_signal(barrier, inc=1, device_id=device, device_id_type=MESH)

    loop(1, 16, lambda d: greet((s, lax.rem(e + d, 16))))
    loop(1, 8, lambda d: greet((lax.rem(s + d, 8), e)))
    greet((s_next, mate))
    greet((s_last, mate))

    loads[0].wait()
    kext[parity, 0:32, 128:640] = kraw[...]
    loads[1].wait()
    kext[parity, 32:64, 128:640] = vraw[...]
    pl.semaphore_wait(barrier, 24)
    own_rows = kext.at[parity, :, pl.ds(128, 512)]
    own_tail = kext.at[parity, :, pl.ds(512, 128)]
    prior = kext.at[parity, :, pl.ds(0, 128)]
    kv_copies = [
        remote(own_rows, own_rows, kv_send.at[0], kv_recv.at[0], (s, mate)),
        remote(own_tail, prior, kv_send.at[1], kv_recv.at[1], (s_next, e)),
        remote(own_tail, prior, kv_send.at[2], kv_recv.at[2], (s_next, mate)),
    ]
    for c in kv_copies:
        c.start()

    own_lanes = (
        lax.broadcasted_iota(jnp.int32, (32, 256), 1)
        == lax.broadcasted_iota(jnp.int32, (32, 256), 0) + s * 32
    )
    own_lanes = jnp.where(own_lanes, 1.0, 0.0)
    loads[8].wait()
    loads[9].wait()
    for part, ref in ((slice(0, 4), ids_ref), (slice(4, 8), gates_ref)):
        metas[s, part, :] = jnp.dot(
            ref[...].astype(F32), own_lanes, preferred_element_type=F32, precision=lax.Precision.HIGHEST
        )

    def meta_copy(d):
        return remote(metas.at[s], metas.at[s], meta_send.at[0], meta_recv.at[0], (lax.rem(s + d, 8), e))

    loop(1, 8, lambda d: meta_copy(d).start())

    bdk[...] = jnp.zeros((4, 128, 512), BF)
    bdv[...] = jnp.zeros((4, 128, 512), BF)
    loads[2].wait()
    loads[3].wait()
    for c in kv_copies:
        c.wait_recv()

    query_pos = lax.broadcasted_iota(jnp.int32, (128, 256), 0)
    key_pos = lax.broadcasted_iota(jnp.int32, (128, 256), 1)
    inside = (key_pos > query_pos) & (key_pos <= query_pos + 128)

    def attend(b):
        window = pl.ds(aligned(b * 128, 128), 256)
        for half in range(2):
            for p in range(2):
                rows = slice(half * 64 + p * 32, half * 64 + p * 32 + 32)
                bdk[b, rows, half * 256 : half * 256 + 256] = kext[p, 0:32, window]
                bdv[b, rows, half * 256 : half * 256 + 256] = kext[p, 32:64, window]
        allowed = inside & (key_pos + (s * 512 + b * 128) >= 128)
        for pair in range(2):
            queries = q[pl.ds(aligned(b * 128, 128), 128), pair * 128 : pair * 128 + 128]
            scores = mm(queries, bdk[b]) * (1.0 / math.sqrt(64))
            probs = []
            for half in range(2):
                sink = sink_ref[pair * 2 + half]
                part = jnp.where(allowed, scores[:, half * 256 : half * 256 + 256], -1e30)
                highest = jnp.maximum(jnp.max(part, axis=1, keepdims=True), sink)
                raised = jnp.exp(part - highest)
                total = jnp.sum(raised, axis=1, keepdims=True) + jnp.exp(sink - highest)
                probs.append((raised * (1.0 / total)).astype(BF))
            mixed = mm_nt(jnp.concatenate(probs, axis=1), bdv[b])
            att[pl.ds(aligned(b * 128, 128), 128), pair * 128 : pair * 128 + 128] = mixed.astype(BF)

    for b in range(4):
        attend(b)

    def columns(c, widths=WIDTHS):
        return slice(sum(widths[:c]), sum(widths[: c + 1]))

    def tiles(width):
        return [slice(low, min(low + COL, width)) for low in range(0, width, COL)]

    def half_columns(c, half):
        wide = WIDTHS[c] // 2
        return slice(sum(WIDTHS[:c]) + half * wide, sum(WIDTHS[:c]) + half * wide + wide)

    def project(c):
        for half in range(2):
            share = mm(att[...], wo[:, half_columns(c, half)])
            shares[c][half] = share.reshape(4, 128, WIDTHS[c] // 2).astype(BF)
            for i in range(3):
                first_copy(c, half, i).start()

    def z_peer(i):
        return lax.rem(z + 1 + i, 4)

    def x_peer(i):
        return lax.rem(x + 1 + i, 4)

    def rows_of(peer):
        return pl.ds(aligned(peer * 32, 32), 32)

    def first_copy(c, half, i):
        if half == 0:
            src, dst, peer = shares[c].at[0, z_peer(i)], recv_z[c].at[z], z_peer(i) * 4 + x
        else:
            src, dst, peer = shares[c].at[1, :, rows_of(x_peer(i))], recv_x[c].at[x], z * 4 + x_peer(i)
        return remote(src, dst, first_send.at[c, half], first_recv.at[c, half], (s, peer))

    def second_copy(c, half, i):
        if half == 0:
            src, dst, peer = sum_a[c].at[rows_of(x_peer(i))], recv_a2[c].at[x], z * 4 + x_peer(i)
        else:
            src, dst, peer = sum_b[c].at[z_peer(i)], recv_b2[c].at[z], z_peer(i) * 4 + x
        return remote(src, dst, second_send.at[c, half], second_recv.at[c, half], (s, peer))

    def sum_first(c):
        arrived(recv_z[c].at[pl.ds(0, 3)], first_recv.at[c, 0])
        total = shares[c][0, z].astype(F32)
        for i in range(3):
            total = total + recv_z[c][z_peer(i)].astype(F32)
        sum_a[c][...] = total.astype(BF)
        for i in range(3):
            second_copy(c, 0, i).start()
        arrived(recv_x[c].at[pl.ds(0, 3)], first_recv.at[c, 1])
        total = shares[c][1, :, rows_of(x), :].astype(F32)
        for i in range(3):
            total = total + recv_x[c][x_peer(i)].astype(F32)
        sum_b[c][...] = total.astype(BF)
        for i in range(3):
            second_copy(c, 1, i).start()

    own_block = pl.ds(aligned(s * 32, 32), 32)
    own_slots = pl.ds(aligned(e * 16, 16), 16)

    def along_y(k):
        return lax.rem(y + k, 4) * 2 + core

    def gather_copy(c, k):
        block = tokens[c].at[own_block]
        peer = twin if k == 0 else along_y(k)
        return remote(block, block, gather_send.at[c], gather_recv.at[c, k], (peer, e))

    def relay_copy(c, k):
        block = tokens[c].at[pl.ds(aligned(along_y(4 - k) * 32, 32), 32)]
        return remote(block, block, relay_send.at[c], relay_recv.at[c], (twin, e))

    def cross_copy(c):
        return remote(partial[c].at[:, 1 - core], crossed[c], cross_send.at[c], cross_recv.at[c], (twin, e))

    def home_copy(c, k):
        return remote(
            summed[c].at[lax.rem(y + k, 4)],
            returned[c].at[y],
            home_send.at[c],
            home_recv.at[c],
            (along_y(k), e),
        )

    squares = []

    def sum_second(c):
        for half, sums, place, received, peers in (
            (0, sum_a, rows_of(x), recv_a2, x_peer),
            (1, sum_b, z, recv_b2, z_peer),
        ):
            arrived(received[c].at[pl.ds(0, 3)], second_recv.at[c, half])
            here = half_columns(c, half)
            wide = WIDTHS[c] // 2
            total = res[:, here].astype(F32) + sums[c][place].astype(F32)
            for i in range(3):
                total = total + received[c][peers(i)].astype(F32)
            hidden[:, here] = total
            squares.append(jnp.sum(total * total, axis=1, keepdims=True))
            tokens[c][own_block, half * wide : half * wide + wide] = (total * gain[:, here]).astype(BF)
        if c == CHUNKS - 1:
            mean = sum(squares[1:], squares[0]) * (1.0 / D)
            rest = jnp.broadcast_to(lax.rsqrt(mean + 1e-05), (32, EXTRA))
            lane = lax.broadcasted_iota(jnp.int32, (32, EXTRA), 1)
            parts = jnp.zeros((32, EXTRA), F32)
            for i in range(3):
                rounded = rest.astype(BF).astype(F32)
                parts = jnp.where(lane == i, rounded, parts)
                rest = rest - rounded
            tokens[c][own_block, WIDTHS[c] : WIDTHS[c] + EXTRA] = parts.astype(BF)
        for k in (1, 3, 2, 0):
            gather_copy(c, k).start()

    def ex_copy(use, c, d):
        peer = lax.rem(e + d, 16)
        src, dst = (slots[c], rows_in[c]) if use == 0 else (rows_out[c], answers[c])
        return remote(
            src.at[pl.ds(aligned(peer * 16, 16), 16)],
            dst.at[own_slots],
            ex_send.at[use, c],
            ex_recv.at[use, c],
            (s, peer),
        )

    def relay(c):
        for k in (1, 3, 2):
            gather_copy(c, k).wait_recv()
            relay_copy(c, k).start()

    def dispatch(c):
        gather_copy(c, 0).wait_recv()
        arrived(tokens[c].at[pl.ds(0, 96)], relay_recv.at[c])
        for n in tiles(WIDTHS[c] + (EXTRA if c == CHUNKS - 1 else 0)):
            slots[c][:, n] = mm(select[...], tokens[c][:, n]).astype(BF)
        loop(1, 16, lambda d: ex_copy(0, c, d).start())
        rows_in[c][own_slots, :] = slots[c][own_slots, :]

    def up_tile(c, low, width, scale):
        out = pl.ds(aligned(low, 128), width)
        sums = []
        for base, acc in ((0, acc_gate), (FF, acc_lift)):
            weights = wgu[0, pl.ds(aligned(base + low, 16), width), columns(c)]
            tile = mm_nt(rows_in[c][:, 0 : WIDTHS[c]], weights)
            if c > 0:
                tile = tile + acc[:, out]
            if c < CHUNKS - 1:
                acc[:, out] = tile
            sums.append(tile)
        if c == CHUNKS - 1:
            gate, lift = sums[0] * scale, sums[1] * scale
            act[:, out] = (gate * (1.0 / (1.0 + jnp.exp(-1.702 * gate))) * (lift + 1.0)).astype(BF)

    def up(c):
        arrived(rows_in[c].at[pl.ds(0, 240)], ex_recv.at[0, c])
        scale = None
        if c == CHUNKS - 1:
            scale = jnp.sum(rows_in[c][:, WIDTHS[c] : WIDTHS[c] + EXTRA].astype(F32), axis=1, keepdims=True)
        for n in range(5):
            up_tile(c, n * COL, COL, scale)
        up_tile(c, 5 * COL, FF - 5 * COL, scale)

    project(0)
    project(1)
    arrived(metas.at[pl.ds(0, 7)], meta_recv.at[0])
    meta = metas[0]
    for i in range(1, 8):
        meta = meta + metas[i]
    place = lax.broadcasted_iota(jnp.int32, (256, 256), 0)
    token = lax.broadcasted_iota(jnp.int32, (256, 256), 1)
    mine = ((place & 15) >> 1) == (token >> 5)
    expert = ((place >> 4) + s * 16).astype(F32)
    named = jnp.zeros((256, 256), F32)
    weight = jnp.zeros((256, 256), F32)
    for k in range(4):
        same = mine & (meta[k : k + 1, :] == expert)
        named = named + jnp.where(same, 1.0, 0.0)
        weight = weight + jnp.where(same, meta[4 + k : 5 + k, :], 0.0)
    before = jnp.where(place < token, 1.0, 0.0).astype(BF)
    rank = mm(named.astype(BF), before)
    chosen = jnp.where(rank == (place & 1).astype(F32), named, 0.0)
    select[...] = chosen.astype(BF)
    weight = jnp.transpose(weight * chosen)
    high = weight.astype(BF)
    weigh[0] = high
    weigh[1] = (weight - high.astype(F32)).astype(BF)

    loads[4].wait()
    loads[7].wait()
    gain = gain_ref[...].reshape(1, D)
    for c in range(CHUNKS):
        sum_first(c)
        if c + 2 < CHUNKS:
            project(c + 2)
        if c >= 1:
            sum_second(c - 1)
        if c >= 2:
            relay(c - 2)
        if c >= 3:
            dispatch(c - 3)
    sum_second(4)
    for c in range(3, CHUNKS):
        relay(c)
        dispatch(c - 1)
    dispatch(4)
    loads[5].wait()
    for c in range(CHUNKS):
        up(c)

    loads[6].wait()
    for c in range(CHUNKS):
        low = sum(BACK[:c])
        for n in tiles(BACK[c]):
            rows_out[c][:, n] = mm(act[...], wd[0, :, low + n.start : low + n.stop]).astype(BF)
        loop(1, 16, lambda d: ex_copy(1, c, d).start())
        answers[c][own_slots, :] = rows_out[c][own_slots, :]

    def combine(c):
        arrived(answers[c].at[pl.ds(0, 240)], ex_recv.at[1, c])
        for n in tiles(BACK[c]):
            sums = mm(weigh[0], answers[c][:, n]) + mm(weigh[1], answers[c][:, n])
            partial[c][:, :, :, n] = sums.reshape(4, 2, 32, n.stop - n.start).astype(BF)
        cross_copy(c).start()

    def reduce(c):
        cross_copy(c).wait_recv()
        for i in range(4):
            summed[c][i] = (partial[c][i, core].astype(F32) + crossed[c][i].astype(F32)).astype(BF)
        for k in (1, 3, 2):
            home_copy(c, k).start()

    def finish(c):
        total = hidden[:, columns(c, BACK)] + summed[c][y].astype(F32)
        arrived(returned[c].at[pl.ds(0, 3)], home_recv.at[c])
        for k in range(1, 4):
            total = total + returned[c][lax.rem(y + k, 4)].astype(F32)
        out_ref[:, columns(c, BACK)] = total.astype(BF)

    for c in kv_copies:
        c.wait_send()
    arrived(metas.at[pl.ds(0, 7)], meta_send.at[0])
    for c in range(CHUNKS):
        arrived(recv_z[c].at[pl.ds(0, 3)], first_send.at[c, 0])
        arrived(recv_x[c].at[pl.ds(0, 3)], first_send.at[c, 1])
        arrived(recv_a2[c].at[pl.ds(0, 3)], second_send.at[c, 0])
        arrived(recv_b2[c].at[pl.ds(0, 3)], second_send.at[c, 1])
        arrived(tokens[c].at[pl.ds(0, 128)], gather_send.at[c])
        arrived(tokens[c].at[pl.ds(0, 96)], relay_send.at[c])
        arrived(slots[c].at[pl.ds(0, 240)], ex_send.at[0, c])

    combine(0)
    for c in range(1, CHUNKS):
        reduce(c - 1)
        combine(c)
    reduce(CHUNKS - 1)
    for c in range(CHUNKS):
        arrived(rows_out[c].at[pl.ds(0, 240)], ex_send.at[1, c])
        finish(c)

    for c in range(CHUNKS):
        cross_copy(c).wait_send()
        arrived(summed[c].at[pl.ds(0, 3)], home_send.at[c])


def per_device(
    queries, key_rows, value_rows, sink_logits, out_proj, residual, norm_gain, expert_ids, gate_weights,
    w_gate_up, w_down,
):
    hbm = pl.BlockSpec(memory_space=pl.ANY)
    vmem = pl.BlockSpec(memory_space=pltpu.VMEM)
    smem = pl.BlockSpec(memory_space=pltpu.SMEM)
    dma = pltpu.SemaphoreType.DMA

    def chunks(widths, *shape):
        return [pltpu.VMEM((*shape, width), BF) for width in widths]

    halves = [width // 2 for width in WIDTHS]
    carried = [*WIDTHS[:-1], WIDTHS[-1] + EXTRA]
    scratch = [
        pltpu.VMEM((512, 256), BF),
        pltpu.VMEM((32, 512), BF),
        pltpu.VMEM((32, 512), BF),
        pltpu.VMEM((256, D), BF),
        pltpu.VMEM((32, D), BF),
        pltpu.VMEM((1, 2 * FF, D), BF),
        pltpu.VMEM((1, FF, D), BF),
        pltpu.VMEM((D,), F32),
        pltpu.VMEM((4, 32), jnp.int32),
        pltpu.VMEM((4, 32), F32),
        pltpu.VMEM((2, 64, 640), BF),
        pltpu.VMEM((4, 128, 512), BF),
        pltpu.VMEM((4, 128, 512), BF),
        pltpu.VMEM((512, 256), BF),
        pltpu.VMEM((32, D), F32),
        pltpu.VMEM((8, 8, 256), F32),
        pltpu.VMEM((256, 256), BF),
        pltpu.VMEM((2, 256, 256), BF),
        pltpu.VMEM((256, FF), F32),
        pltpu.VMEM((256, FF), F32),
        pltpu.VMEM((256, FF), BF),
        *chunks(halves, 2, 4, 128),
        *chunks(halves, 4, 128),
        *chunks(halves, 4, 4, 32),
        *chunks(halves, 128),
        *chunks(halves, 4, 32),
        *chunks(halves, 4, 32),
        *chunks(halves, 4, 32),
        *chunks(carried, 256) * 3,
        *chunks(BACK, 256) * 2,
        *chunks(BACK, 4, 2, 32),
        *chunks(BACK, 4, 32) * 3,
        dma((10,)),
        dma((3,)),
        dma((3,)),
        *[dma((CHUNKS, 2))] * 4,
        dma((1,)),
        dma((1,)),
        dma((2, CHUNKS)),
        dma((2, CHUNKS)),
        dma((CHUNKS,)),
        dma((CHUNKS, 4)),
        *[dma((CHUNKS,))] * 6,
    ]
    return pl.pallas_call(
        layer_kernel,
        out_shape=jax.ShapeDtypeStruct((32, D), BF),
        in_specs=[hbm, hbm, hbm, smem, hbm, hbm, hbm, hbm, hbm, hbm, hbm],
        out_specs=vmem,
        scratch_shapes=scratch,
        compiler_params=pltpu.CompilerParams(
            collective_id=1, has_side_effects=True, vmem_limit_bytes=60 * 1024 * 1024
        ),
        name="layer",
    )(
        queries, key_rows.T, value_rows.T, sink_logits, out_proj, residual, norm_gain,
        expert_ids.T, gate_weights.T, jnp.swapaxes(w_gate_up, 1, 2), w_down,
    )


def solution(mesh):
    return jax.shard_map(
        per_device,
        mesh=mesh,
        in_specs=(
            P("seq", "exp"),
            P("seq", "exp"),
            P("seq", "exp"),
            P("exp"),
            P("exp", None),
            P(("seq", "exp"), None),
            P(),
            P(("seq", "exp"), None),
            P(("seq", "exp"), None),
            P(("seq", "exp"), None, None),
            P(("seq", "exp"), None, None),
        ),
        out_specs=P(("seq", "exp"), None),
        check_vma=False,
    )
```

```python
import math

import jax
import jax.numpy as jnp
from jax import lax
from jax.experimental import pallas as pl
from jax.experimental.pallas import tpu as pltpu
from jax.sharding import PartitionSpec as P

MESH = pl.DeviceIdType.MESH
BF = jnp.bfloat16
F32 = jnp.float32
D = 2560
FF = 1440
COL = 256
EXTRA = 128
WIDTHS = (256, 512, 512, 512, 512, 256)
BACK = (256, 512, 512, 512, 512, 256)
CHUNKS = len(WIDTHS)
ORDER = (
    "P0", "P1", "P2", "P3", "M0", "M1", "M2", "M3", "S0", "P4", "S1", "P5", "S2", "S3", "T0",
    "M4", "T1", "M5", "R0", "T2", "T3", "S4", "G0", "S5", "R1", "R2", "T4", "G1", "R3", "G2",
    "T5", "G3", "R4", "R5", "G4", "G5",
)


def mm(a, b):
    return jnp.dot(a, b, preferred_element_type=F32)


def mm_nt(a, b):
    return lax.dot_general(a, b, (((1,), (1,)), ((), ())), preferred_element_type=F32)


def remote(src, dst, send_sem, recv_sem, device):
    return pltpu.make_async_remote_copy(
        src, dst, send_sem, recv_sem, device_id=device, device_id_type=MESH
    )


def aligned(value, multiple):
    return pl.multiple_of(value, multiple)


def arrived(parts, sem):
    pltpu.make_async_copy(parts, parts, sem).wait()


def loop(low, high, body):
    def step(i, carry):
        body(i)
        return carry

    lax.fori_loop(low, high, step, 0)


def layer_kernel(
    q_hbm, k_hbm, v_hbm, sink_hbm, wo_hbm, res_hbm, gain_hbm, ids_hbm, gates_hbm, wgu_hbm, wd_hbm, out_ref, *scratch
):
    take = iter(scratch)

    def per_chunk():
        return [next(take) for _ in range(CHUNKS)]

    q, kraw, vraw, wo, res, wgu, wd, gain_ref, ids_ref, gates_ref, sinks = [next(take) for _ in range(11)]
    kext, bdk, bdv, att, hidden, metas, select, weigh, acc_gate, acc_lift, act = [next(take) for _ in range(11)]
    shares, via_a, via_b, recv_z, recv_x, sum_a, sum_b, recv_a2, recv_b2 = [per_chunk() for _ in range(9)]
    via = (via_a, via_b)
    tokens, slots, rows_in = [per_chunk() for _ in range(3)]
    rows_out, answers, partial, crossed, summed, returned = [per_chunk() for _ in range(6)]
    load_sem, kv_send, kv_recv, via_send, via_recv, first_send, first_recv = [next(take) for _ in range(7)]
    second_send, second_recv, meta_send, meta_recv, ex_send, ex_recv, gather_send, gather_recv = [next(take) for _ in range(8)]
    relay_send, relay_recv, cross_send, cross_recv, home_send, home_recv = [next(take) for _ in range(6)]
    s = lax.axis_index("seq")
    e = lax.axis_index("exp")
    z = e // 4
    x = lax.rem(e, 4)
    parity = lax.rem(e, 2)
    mate = e + 1 - 2 * parity
    y = s // 2
    core = lax.rem(s, 2)
    twin = s + 1 - 2 * core
    s_next = lax.rem(s + 1, 8)
    s_last = lax.rem(s + 7, 8)

    barrier = pltpu.get_barrier_semaphore()

    def greet(device):
        pl.semaphore_signal(barrier, inc=1, device_id=device, device_id_type=MESH)

    loop(1, 16, lambda d: greet((s, lax.rem(e + d, 16))))
    loop(1, 8, lambda d: greet((lax.rem(s + d, 8), e)))
    greet((s_next, mate))
    greet((s_last, mate))

    loads = [
        pltpu.make_async_copy(a, b, load_sem.at[i])
        for i, (a, b) in enumerate(
            [
                (k_hbm, kraw), (v_hbm, vraw), (q_hbm, q), (wo_hbm, wo), (res_hbm, res), (wgu_hbm, wgu), (wd_hbm, wd),
                (gain_hbm, gain_ref), (ids_hbm, ids_ref), (gates_hbm, gates_ref), (sink_hbm, sinks),
            ]
        )
    ]
    for i in (0, 1, 2, 10, 8, 9, 3, 7, 4, 5, 6):
        loads[i].start()

    loads[0].wait()
    kext[parity, 0:32, 128:640] = kraw[...]
    loads[1].wait()
    kext[parity, 32:64, 128:640] = vraw[...]
    pl.semaphore_wait(barrier, 24)
    own_rows = kext.at[parity, :, pl.ds(128, 512)]
    own_tail = kext.at[parity, :, pl.ds(512, 128)]
    prior = kext.at[parity, :, pl.ds(0, 128)]
    kv_copies = [
        remote(own_rows, own_rows, kv_send.at[0], kv_recv.at[0], (s, mate)),
        remote(own_tail, prior, kv_send.at[1], kv_recv.at[1], (s_next, e)),
        remote(own_tail, prior, kv_send.at[2], kv_recv.at[2], (s_next, mate)),
    ]
    for c in kv_copies:
        c.start()

    own_lanes = (
        lax.broadcasted_iota(jnp.int32, (32, 256), 1)
        == lax.broadcasted_iota(jnp.int32, (32, 256), 0) + s * 32
    )
    own_lanes = jnp.where(own_lanes, 1.0, 0.0)
    loads[8].wait()
    loads[9].wait()
    for part, ref in ((slice(0, 4), ids_ref), (slice(4, 8), gates_ref)):
        metas[s, part, :] = jnp.dot(
            ref[...].astype(F32), own_lanes, preferred_element_type=F32, precision=lax.Precision.HIGHEST
        )

    def meta_copy(d):
        return remote(metas.at[s], metas.at[s], meta_send.at[0], meta_recv.at[0], (lax.rem(s + d, 8), e))

    loop(1, 8, lambda d: meta_copy(d).start())

    bdk[...] = jnp.zeros((4, 128, 512), BF)
    bdv[...] = jnp.zeros((4, 128, 512), BF)
    for i in (2, 3, 10):
        loads[i].wait()
    for c in kv_copies:
        c.wait_recv()

    query_pos = lax.broadcasted_iota(jnp.int32, (128, 256), 0)
    key_pos = lax.broadcasted_iota(jnp.int32, (128, 256), 1)
    inside = (key_pos > query_pos) & (key_pos <= query_pos + 128)

    def attend(b):
        window = pl.ds(aligned(b * 128, 128), 256)
        for half in range(2):
            for p in range(2):
                rows = slice(half * 64 + p * 32, half * 64 + p * 32 + 32)
                bdk[b, rows, half * 256 : half * 256 + 256] = kext[p, 0:32, window]
                bdv[b, rows, half * 256 : half * 256 + 256] = kext[p, 32:64, window]
        allowed = inside & (key_pos + (s * 512 + b * 128) >= 128)
        for pair in range(2):
            queries = q[pl.ds(aligned(b * 128, 128), 128), pair * 128 : pair * 128 + 128]
            scores = mm(queries, bdk[b]) * (1.0 / math.sqrt(64))
            probs = []
            for half in range(2):
                sink = sinks[pair * 2 + half]
                part = jnp.where(allowed, scores[:, half * 256 : half * 256 + 256], -1e30)
                highest = jnp.maximum(jnp.max(part, axis=1, keepdims=True), sink)
                raised = jnp.exp(part - highest)
                total = jnp.sum(raised, axis=1, keepdims=True) + jnp.exp(sink - highest)
                probs.append((raised * (1.0 / total)).astype(BF))
            mixed = mm_nt(jnp.concatenate(probs, axis=1), bdv[b])
            att[pl.ds(aligned(b * 128, 128), 128), pair * 128 : pair * 128 + 128] = mixed.astype(BF)

    for b in range(4):
        attend(b)

    def columns(c, widths=WIDTHS):
        return slice(sum(widths[:c]), sum(widths[: c + 1]))

    def tiles(width):
        return [slice(low, min(low + COL, width)) for low in range(0, width, COL)]

    def half_columns(c, half):
        wide = WIDTHS[c] // 2
        return slice(sum(WIDTHS[:c]) + half * wide, sum(WIDTHS[:c]) + half * wide + wide)

    def z_peer(i):
        return lax.rem(z + 1 + i, 4)

    def x_peer(i):
        return lax.rem(x + 1 + i, 4)

    def rows_of(peer):
        return pl.ds(aligned(peer * 32, 32), 32)

    def piece(c, half, i):
        return shares[c].at[0, z_peer(i)] if half == 0 else shares[c].at[1, :, rows_of(x_peer(i))]

    def part_of(half, ref, p):
        return ref.at[pl.ds(p * 64, 64)] if half == 0 else ref.at[pl.ds(p * 2, 2)]

    def neighbour(half, side):
        i = 2 * side
        return (s, z_peer(i) * 4 + x) if half == 0 else (s, z * 4 + x_peer(i))

    def via_copy(c, half, p):
        src = part_of(half, piece(c, half, 1), p)
        return remote(src, via[half][c].at[p], via_send.at[c, half], via_recv.at[c, half], neighbour(half, p))

    def near_copy(c, half, side, p):
        src = part_of(half, piece(c, half, 2 * side), p)
        dst = part_of(half, (recv_z, recv_x)[half][c].at[side], p)
        return remote(src, dst, first_send.at[c, half], first_recv.at[c, half], neighbour(half, side))

    def project(c):
        for half in range(2):
            share = mm(att[...], wo[:, half_columns(c, half)])
            shares[c][half] = share.reshape(4, 128, WIDTHS[c] // 2).astype(BF)
            for p in range(2):
                via_copy(c, half, p).start()
            for p in range(2):
                near_copy(c, half, 1 - p, p).start()

    def merge(c):
        for half in range(2):
            arrived(via[half][c], via_recv.at[c, half])
            for p in range(2):
                own = part_of(half, piece(c, half, 2 * p), p)
                own[...] = (own[...].astype(F32) + via[half][c][p].astype(F32)).astype(BF)
                near_copy(c, half, p, p).start()

    def second_copy(c, half, i):
        if half == 0:
            src, dst, peer = sum_a[c].at[rows_of(x_peer(i))], recv_a2[c].at[x], z * 4 + x_peer(i)
        else:
            src, dst, peer = sum_b[c].at[z_peer(i)], recv_b2[c].at[z], z_peer(i) * 4 + x
        return remote(src, dst, second_send.at[c, half], second_recv.at[c, half], (s, peer))

    def sum_first(c):
        arrived(recv_z[c], first_recv.at[c, 0])
        total = shares[c][0, z].astype(F32)
        for side in range(2):
            total = total + recv_z[c][side].astype(F32)
        sum_a[c][...] = total.astype(BF)
        for i in range(3):
            second_copy(c, 0, i).start()
        arrived(recv_x[c], first_recv.at[c, 1])
        total = shares[c][1, :, rows_of(x), :].astype(F32)
        for side in range(2):
            total = total + recv_x[c][side].astype(F32)
        sum_b[c][...] = total.astype(BF)
        for i in range(3):
            second_copy(c, 1, i).start()

    own_block = pl.ds(aligned(s * 32, 32), 32)
    own_slots = pl.ds(aligned(e * 16, 16), 16)

    def along_y(k):
        return lax.rem(y + k, 4) * 2 + core

    def gather_copy(c, k):
        block = tokens[c].at[own_block]
        peer = twin if k == 0 else along_y(k)
        return remote(block, block, gather_send.at[c], gather_recv.at[c, k], (peer, e))

    def relay_copy(c, k):
        block = tokens[c].at[pl.ds(aligned(along_y(4 - k) * 32, 32), 32)]
        return remote(block, block, relay_send.at[c], relay_recv.at[c], (twin, e))

    def cross_copy(c):
        return remote(partial[c].at[:, 1 - core], crossed[c], cross_send.at[c], cross_recv.at[c], (twin, e))

    def home_copy(c, k):
        return remote(
            summed[c].at[lax.rem(y + k, 4)],
            returned[c].at[y],
            home_send.at[c],
            home_recv.at[c],
            (along_y(k), e),
        )

    squares = []

    def sum_second(c):
        for half, sums, place, received, peers in (
            (0, sum_a, rows_of(x), recv_a2, x_peer),
            (1, sum_b, z, recv_b2, z_peer),
        ):
            arrived(received[c].at[pl.ds(0, 3)], second_recv.at[c, half])
            here = half_columns(c, half)
            wide = WIDTHS[c] // 2
            total = res[:, here].astype(F32) + sums[c][place].astype(F32)
            for i in range(3):
                total = total + received[c][peers(i)].astype(F32)
            hidden[:, here] = total
            squares.append(jnp.sum(total * total, axis=1, keepdims=True))
            tokens[c][own_block, half * wide : half * wide + wide] = (total * gain[:, here]).astype(BF)
        if c == CHUNKS - 1:
            mean = sum(squares[1:], squares[0]) * (1.0 / D)
            rest = jnp.broadcast_to(lax.rsqrt(mean + 1e-05), (32, EXTRA))
            lane = lax.broadcasted_iota(jnp.int32, (32, EXTRA), 1)
            parts = jnp.zeros((32, EXTRA), F32)
            for i in range(3):
                rounded = rest.astype(BF).astype(F32)
                parts = jnp.where(lane == i, rounded, parts)
                rest = rest - rounded
            tokens[c][own_block, WIDTHS[c] : WIDTHS[c] + EXTRA] = parts.astype(BF)
        for k in (1, 3, 2, 0):
            gather_copy(c, k).start()

    def ex_copy(use, c, d):
        peer = lax.rem(e + d, 16)
        src, dst = (slots[c], rows_in[c]) if use == 0 else (rows_out[c], answers[c])
        return remote(
            src.at[pl.ds(aligned(peer * 16, 16), 16)],
            dst.at[own_slots],
            ex_send.at[use, c],
            ex_recv.at[use, c],
            (s, peer),
        )

    def relay(c):
        for k in (1, 3, 2):
            gather_copy(c, k).wait_recv()
            relay_copy(c, k).start()

    def dispatch(c):
        gather_copy(c, 0).wait_recv()
        arrived(tokens[c].at[pl.ds(0, 96)], relay_recv.at[c])
        for n in tiles(WIDTHS[c] + (EXTRA if c == CHUNKS - 1 else 0)):
            slots[c][:, n] = mm(select[...], tokens[c][:, n]).astype(BF)
        loop(1, 16, lambda d: ex_copy(0, c, d).start())
        rows_in[c][own_slots, :] = slots[c][own_slots, :]

    def up_tile(c, low, width, scale):
        out = pl.ds(aligned(low, 128), width)
        sums = []
        for base, acc in ((0, acc_gate), (FF, acc_lift)):
            weights = wgu[0, pl.ds(aligned(base + low, 16), width), columns(c)]
            tile = mm_nt(rows_in[c][:, 0 : WIDTHS[c]], weights)
            if c > 0:
                tile = tile + acc[:, out]
            if c < CHUNKS - 1:
                acc[:, out] = tile
            sums.append(tile)
        if c == CHUNKS - 1:
            gate, lift = sums[0] * scale, sums[1] * scale
            act[:, out] = (gate * (1.0 / (1.0 + jnp.exp(-1.702 * gate))) * (lift + 1.0)).astype(BF)

    def up(c):
        arrived(rows_in[c].at[pl.ds(0, 240)], ex_recv.at[0, c])
        scale = None
        if c == CHUNKS - 1:
            scale = jnp.sum(rows_in[c][:, WIDTHS[c] : WIDTHS[c] + EXTRA].astype(F32), axis=1, keepdims=True)
        for n in range(5):
            up_tile(c, n * COL, COL, scale)
        up_tile(c, 5 * COL, FF - 5 * COL, scale)

    def run(names):
        steps = {"P": project, "M": merge, "S": sum_first, "T": sum_second, "R": relay, "G": dispatch}
        for name in names:
            steps[name[0]](int(name[1]))

    run(ORDER[:2])

    arrived(metas.at[pl.ds(0, 7)], meta_recv.at[0])
    meta = metas[0]
    for i in range(1, 8):
        meta = meta + metas[i]
    place = lax.broadcasted_iota(jnp.int32, (256, 256), 0)
    token = lax.broadcasted_iota(jnp.int32, (256, 256), 1)
    mine = ((place & 15) >> 1) == (token >> 5)
    expert = ((place >> 4) + s * 16).astype(F32)
    named = jnp.zeros((256, 256), F32)
    weight = jnp.zeros((256, 256), F32)
    for k in range(4):
        same = mine & (meta[k : k + 1, :] == expert)
        named = named + jnp.where(same, 1.0, 0.0)
        weight = weight + jnp.where(same, meta[4 + k : 5 + k, :], 0.0)
    before = jnp.where(place < token, 1.0, 0.0).astype(BF)
    rank = mm(named.astype(BF), before)
    chosen = jnp.where(rank == (place & 1).astype(F32), named, 0.0)
    select[...] = chosen.astype(BF)
    weight = jnp.transpose(weight * chosen)
    high = weight.astype(BF)
    weigh[0] = high
    weigh[1] = (weight - high.astype(F32)).astype(BF)

    loads[4].wait()
    loads[7].wait()
    gain = gain_ref[...].reshape(1, D)
    run(ORDER[2:])
    loads[5].wait()
    for c in range(CHUNKS):
        up(c)

    loads[6].wait()
    for c in range(CHUNKS):
        low = sum(BACK[:c])
        for n in tiles(BACK[c]):
            rows_out[c][:, n] = mm(act[...], wd[0, :, low + n.start : low + n.stop]).astype(BF)
        loop(1, 16, lambda d: ex_copy(1, c, d).start())
        answers[c][own_slots, :] = rows_out[c][own_slots, :]

    def combine(c):
        arrived(answers[c].at[pl.ds(0, 240)], ex_recv.at[1, c])
        for n in tiles(BACK[c]):
            sums = mm(weigh[0], answers[c][:, n]) + mm(weigh[1], answers[c][:, n])
            partial[c][:, :, :, n] = sums.reshape(4, 2, 32, n.stop - n.start).astype(BF)
        cross_copy(c).start()

    def reduce(c):
        cross_copy(c).wait_recv()
        for i in range(4):
            summed[c][i] = (partial[c][i, core].astype(F32) + crossed[c][i].astype(F32)).astype(BF)
        for k in (1, 3, 2):
            home_copy(c, k).start()

    def finish(c):
        total = hidden[:, columns(c, BACK)] + summed[c][y].astype(F32)
        arrived(returned[c].at[pl.ds(0, 3)], home_recv.at[c])
        for k in range(1, 4):
            total = total + returned[c][lax.rem(y + k, 4)].astype(F32)
        out_ref[:, columns(c, BACK)] = total.astype(BF)

    for c in kv_copies:
        c.wait_send()
    arrived(metas.at[pl.ds(0, 7)], meta_send.at[0])
    for c in range(CHUNKS):
        arrived(recv_z[c], first_send.at[c, 0])
        arrived(recv_x[c], first_send.at[c, 1])
        for half in range(2):
            arrived(via[half][c], via_send.at[c, half])
        arrived(recv_a2[c].at[pl.ds(0, 3)], second_send.at[c, 0])
        arrived(recv_b2[c].at[pl.ds(0, 3)], second_send.at[c, 1])
        arrived(tokens[c].at[pl.ds(0, 128)], gather_send.at[c])
        arrived(tokens[c].at[pl.ds(0, 96)], relay_send.at[c])
        arrived(slots[c].at[pl.ds(0, 240)], ex_send.at[0, c])

    combine(0)
    for c in range(1, CHUNKS):
        reduce(c - 1)
        combine(c)
    reduce(CHUNKS - 1)
    for c in range(CHUNKS):
        arrived(rows_out[c].at[pl.ds(0, 240)], ex_send.at[1, c])
        finish(c)

    for c in range(CHUNKS):
        cross_copy(c).wait_send()
        arrived(summed[c].at[pl.ds(0, 3)], home_send.at[c])


def per_device(
    queries, key_rows, value_rows, sink_logits, out_proj, residual, norm_gain, expert_ids, gate_weights,
    w_gate_up, w_down,
):
    hbm = pl.BlockSpec(memory_space=pl.ANY)
    vmem = pl.BlockSpec(memory_space=pltpu.VMEM)
    dma = pltpu.SemaphoreType.DMA

    def chunks(widths, *shape):
        return [pltpu.VMEM((*shape, width), BF) for width in widths]

    halves = [width // 2 for width in WIDTHS]
    carried = [*WIDTHS[:-1], WIDTHS[-1] + EXTRA]
    scratch = [
        pltpu.VMEM((512, 256), BF),
        pltpu.VMEM((32, 512), BF),
        pltpu.VMEM((32, 512), BF),
        pltpu.VMEM((256, D), BF),
        pltpu.VMEM((32, D), BF),
        pltpu.VMEM((1, 2 * FF, D), BF),
        pltpu.VMEM((1, FF, D), BF),
        pltpu.VMEM((D,), F32),
        pltpu.VMEM((4, 32), jnp.int32),
        pltpu.VMEM((4, 32), F32),
        pltpu.SMEM((4,), F32),
        pltpu.VMEM((2, 64, 640), BF),
        pltpu.VMEM((4, 128, 512), BF),
        pltpu.VMEM((4, 128, 512), BF),
        pltpu.VMEM((512, 256), BF),
        pltpu.VMEM((32, D), F32),
        pltpu.VMEM((8, 8, 256), F32),
        pltpu.VMEM((256, 256), BF),
        pltpu.VMEM((2, 256, 256), BF),
        pltpu.VMEM((256, FF), F32),
        pltpu.VMEM((256, FF), F32),
        pltpu.VMEM((256, FF), BF),
        *chunks(halves, 2, 4, 128),
        *chunks(halves, 2, 64),
        *chunks(halves, 2, 2, 32),
        *chunks(halves, 2, 128),
        *chunks(halves, 2, 4, 32),
        *chunks(halves, 128),
        *chunks(halves, 4, 32),
        *chunks(halves, 4, 32),
        *chunks(halves, 4, 32),
        *chunks(carried, 256) * 3,
        *chunks(BACK, 256) * 2,
        *chunks(BACK, 4, 2, 32),
        *chunks(BACK, 4, 32) * 3,
        dma((11,)),
        dma((3,)),
        dma((3,)),
        *[dma((CHUNKS, 2))] * 6,
        dma((1,)),
        dma((1,)),
        dma((2, CHUNKS)),
        dma((2, CHUNKS)),
        dma((CHUNKS,)),
        dma((CHUNKS, 4)),
        *[dma((CHUNKS,))] * 6,
    ]
    return pl.pallas_call(
        layer_kernel,
        out_shape=pltpu.VMEM((32, D), BF),
        in_specs=[hbm, hbm, hbm, hbm, hbm, hbm, hbm, hbm, hbm, hbm, hbm],
        out_specs=vmem,
        scratch_shapes=scratch,
        compiler_params=pltpu.CompilerParams(
            collective_id=1, has_side_effects=True, vmem_limit_bytes=60 * 1024 * 1024
        ),
        name="layer",
    )(
        queries, key_rows.T, value_rows.T, sink_logits, out_proj, residual, norm_gain,
        expert_ids.T, gate_weights.T, jnp.swapaxes(w_gate_up, 1, 2), w_down,
    )


def solution(mesh):
    return jax.shard_map(
        per_device,
        mesh=mesh,
        in_specs=(
            P("seq", "exp"),
            P("seq", "exp"),
            P("seq", "exp"),
            P("exp"),
            P("exp", None),
            P(("seq", "exp"), None),
            P(),
            P(("seq", "exp"), None),
            P(("seq", "exp"), None),
            P(("seq", "exp"), None, None),
            P(("seq", "exp"), None, None),
        ),
        out_specs=P(("seq", "exp"), None),
        check_vma=False,
    )
```
